1024 devices in a mesh: group: 16 (over x, core), seq: 32 (over z_hi, y), tp: 2 (over z_lo).
Axes of the slice: x: 8, y: 8, z: 8 (z_hi: 4, z_lo: 2; z = z_hi * 2 + z_lo), core: 2. Of those that a mesh axis runs over, the one named last changes fastest.
Arguments:
- queries: bfloat16 [32, 2048, 4096], P('seq', 'group', 'tp'), may hold values from -256 to 256
- keys: bfloat16 [32, 2048, 512], P('seq', 'group', 'tp'), may hold values from -12 to 12
- values: bfloat16 [32, 2048, 512], P('seq', 'group', 'tp'), may hold values from -6 to 6
- moe_x: bfloat16 [16, 1024, 2048], P('group', ('seq', 'tp')), may hold values from -6 to 6
- expert_ids: int32 [16, 1024, 8], P('group', ('seq', 'tp')), may hold values from 0 to 63, all different within a row; in each aligned block of 16 rows (0 to 15, 16 to 31, ..., all dimensions but the last counted through in order) at most 3 rows name the same one
- gates: float32 [16, 1024, 8], P('group', ('seq', 'tp')), may hold values from 0.05 to 0.5
- grad_out: bfloat16 [16, 1024, 2048], P('group', ('seq', 'tp')), may hold values from -6 to 6
- w_gate: bfloat16 [64, 2048, 384], P(('seq', 'tp')), may hold values from -0.125 to 0.125
- w_up: bfloat16 [64, 2048, 384], P(('seq', 'tp')), may hold values from -0.125 to 0.125
- w_down: bfloat16 [64, 384, 2048], P(('seq', 'tp')), may hold values from -0.3125 to 0.3125
Outputs:
- attn_out: bfloat16 [32, 2048, 4096], P('seq', 'group', 'tp')
- moe_out: bfloat16 [16, 1024, 2048], P('group', ('seq', 'tp'))
- moe_grad_in: bfloat16 [16, 1024, 2048], P('group', ('seq', 'tp'))
The draws below stay inside these ranges and needn't reach their ends.
Inputs may be any that keep to these rules, and one draw needn't show every extreme that they name: `expert_ids`: each token names 8 different experts. Within each aligned block of 16 tokens (the tokens of one device, in order), no expert is named by more than 3 tokens, and in every draw some block names some expert exactly 3 times.
All inputs are finite; a program needn't handle non-finite values.
Results may differ from the reference program's by a relative error of at most 0.0064.
Values may be sent and summed in bfloat16 or wider, within the bound.
A program may use at most 32 MiB of HBM per device.

```python
import math
import jax
import jax.numpy as jnp
import numpy as np
from jax import lax

D = 2048
H = 32
KVH = 4
HD = 128
TOPK = 8
EXPERTS = 64
FFE = 384
MOE_TOK = 16
CAP = 3
SEQ = 2048
BATCH = 32
GROUP_TOK = 1024
N_GROUP = 16
N_SEQ = 32
N_TP = 2


def drawn_pair(key):
    base_key = jax.random.fold_in(key, 7)
    key_part, query_part = jax.random.split(base_key, 2)
    key_rows = jax.random.truncated_normal(key_part, -4.0, 4.0, (BATCH, SEQ, KVH, HD), jnp.float32)
    query_rows = jax.random.truncated_normal(query_part, -4.0, 4.0, (BATCH, SEQ, H, HD), jnp.float32)
    return (key_rows, query_rows)


def draw_queries(key, part):
    key_rows, query_rows = drawn_pair(key)
    return query_rows.reshape(BATCH, SEQ, H * HD).astype(jnp.bfloat16)


def draw_keys(key, part):
    key_rows, query_rows = drawn_pair(key)
    return key_rows.reshape(BATCH, SEQ, KVH * HD).astype(jnp.bfloat16)


def levels(own_key, extent, cuts, low, largest):
    def one(axis_at, blocks):
        draws = jax.random.uniform(jax.random.fold_in(jax.random.fold_in(own_key, 6), axis_at), (blocks,), jnp.float32, low / len(cuts), largest / len(cuts))
        return jnp.repeat(jnp.exp(draws), extent[axis_at] // blocks).reshape((-1,) + (1,) * (len(extent) - axis_at - 1))

    factor_of = one(*cuts[0])
    for cut in cuts[1:]:
        factor_of = factor_of * one(*cut)
    return factor_of


def deal_out(key, own, number, rows, amount, top, bound, lean):
    ranking = jax.random.permutation(key, amount)
    heavy_load, common = shares(amount, rows * top, bound, lean, True), shares(amount, rows * top, bound, lean, False)
    places = jnp.arange(amount)

    def named(tallies, offset_by):
        used = int((tallies > 0).sum())
        fixed = max(1, used // 4)
        moved = fixed + (places - fixed + offset_by * (used - fixed)) % max(1, amount - fixed)
        return jnp.zeros((amount,), jnp.int32).at[ranking[jnp.where(places < fixed, places, moved)]].set(jnp.asarray(tallies, jnp.int32))

    tallies = jnp.where(number % 4 == 0, named(heavy_load, number // 4), named(common, number - number // 4 - 1))
    mixed = jax.random.permutation(jax.random.fold_in(own, 3), amount)
    donor, taker = mixed[0:amount // 2 * 2:2], mixed[1:amount // 2 * 2:2]
    slack = jnp.minimum(tallies[donor] - 1, bound - tallies[taker]) // 2
    slack = jnp.where((donor == ranking[0]) | (taker == ranking[0]) | (tallies[taker] == 0), 0, jnp.maximum(slack, 0))
    moved = jax.random.randint(jax.random.fold_in(own, 4), (amount // 2,), 0, 1 << 20) % (slack + 1)
    tallies = tallies.at[donor].add(-moved).at[taker].add(moved)
    members = jnp.searchsorted(jnp.cumsum(tallies), jnp.arange(rows * top), side="right").astype(jnp.int32)
    listing = members.reshape(top, rows).T
    listing = listing[jax.random.permutation(jax.random.fold_in(own, 1), rows)]
    offset_by = jax.random.randint(jax.random.fold_in(own, 2), (rows, 1), 0, top)
    return jnp.take_along_axis(listing, (jnp.arange(top)[None, :] + offset_by) % top, axis=1)


def shares(number_of, total, reach, lean, full):
    portions = [(1 << 20) // math.isqrt(grade ** lean) + 1 for grade in range(1, number_of + 1)]
    largest = reach if full else min(reach, max(-(-total // number_of), total * portions[0] // sum(portions)))
    least = 1 if total - largest >= number_of - 1 else 0
    given, surplus = [largest] + [least] * (number_of - 1), total - largest - least * (number_of - 1)
    while surplus > 0:
        free = [i for i in range(1, number_of) if given[i] < largest] or [i for i in range(1, number_of) if given[i] < reach]
        pool, budget = sum([portions[i] for i in free]), surplus
        for i in free:
            more = min(reach - given[i], max(1, budget * portions[i] // pool), surplus)
            given[i] = given[i] + more
            surplus = surplus - more
    return np.array(given)


def gaussian(own_key, shape, scale, most, cuts=(), held_as=jnp.bfloat16):
    loudness = levels(own_key, shape, cuts, -0.22, 0.18) if cuts else 1.0
    array = jax.random.normal(own_key, shape, jnp.float32) * scale * loudness
    return jnp.minimum(jnp.maximum(array, -most), most).astype(held_as)


def setup_inputs(seed: int = 0) -> dict:
    streams_of = jax.random.split(jax.random.key(seed), 11)
    queries = draw_queries(jax.random.fold_in(streams_of[10], 71), 0)
    keys = draw_keys(jax.random.fold_in(streams_of[10], 71), 0)
    values = gaussian(streams_of[2], (BATCH, SEQ, KVH * HD), 1.0, 6.0, ((0, 32), (1, 16), (2, 2)))
    moe_x = gaussian(streams_of[3], (N_GROUP, GROUP_TOK, D), 1.0, 6.0, ((0, 16), (1, 64)))
    expert_ids_keys = jax.random.split(jax.random.fold_in(streams_of[4], 1), N_GROUP * GROUP_TOK // MOE_TOK)
    expert_ids_turns = jax.random.permutation(jax.random.fold_in(streams_of[4], 3), N_GROUP * GROUP_TOK // MOE_TOK)
    expert_ids = jax.vmap(lambda own, number: deal_out(jax.random.fold_in(streams_of[4], 2), own, number, MOE_TOK, EXPERTS, TOPK, CAP, 2))(expert_ids_keys, expert_ids_turns).reshape((N_GROUP, GROUP_TOK, TOPK))
    gates = jnp.clip(jnp.exp(math.log(0.5) - 2.3025851 * jax.random.uniform(streams_of[5], (N_GROUP, GROUP_TOK, TOPK), jnp.float32) ** levels(streams_of[5], (N_GROUP, GROUP_TOK, TOPK), ((0, 16), (1, 64)), -0.2, 0.2)), 0.05, 0.5)
    grad_out = gaussian(streams_of[6], (N_GROUP, GROUP_TOK, D), 1.0, 6.0, ((0, 16), (1, 64)))
    w_gate = gaussian(streams_of[7], (EXPERTS, D, FFE), D ** -0.5, 0.125, ((0, 64),))
    w_up = gaussian(streams_of[8], (EXPERTS, D, FFE), D ** -0.5, 0.125, ((0, 64),))
    w_down = gaussian(streams_of[9], (EXPERTS, FFE, D), FFE ** -0.5, 0.3125, ((0, 64),))
    return {"queries": queries, "keys": keys, "values": values, "moe_x": moe_x, "expert_ids": expert_ids, "gates": gates, "grad_out": grad_out, "w_gate": w_gate, "w_up": w_up, "w_down": w_down}


def attend_head(query_rows, key_rows, value_rows):
    seq_len = query_rows.shape[0]
    block_len = min(512, seq_len)
    score_scale = 1.0 / (query_rows.shape[1] ** 0.5)
    pieces = []
    for first_row in range(0, seq_len, block_len):
        last_row = first_row + block_len
        scores = lax.dot_general(query_rows[first_row:last_row], key_rows[:last_row], (((1,), (1,)), ((), ())), preferred_element_type=jnp.float32) * score_scale
        row_pos = first_row + lax.broadcasted_iota(jnp.int32, (block_len, last_row), 0)
        col_pos = lax.broadcasted_iota(jnp.int32, (block_len, last_row), 1)
        scores = jnp.where(col_pos <= row_pos, scores, -jnp.inf)
        row_max = jnp.max(scores, axis=1, keepdims=True)
        exp_scores = jnp.exp(scores - row_max)
        row_total = jnp.sum(exp_scores, axis=1, keepdims=True)
        mixed_rows = jnp.dot(exp_scores.astype(jnp.bfloat16), value_rows[:last_row], preferred_element_type=jnp.float32)
        pieces.append((mixed_rows / row_total).astype(jnp.bfloat16))
    return jnp.concatenate(pieces, axis=0)


def attention(queries, keys, values):
    group_len = H // KVH

    def one_head(flat_index):
        batch_idx = flat_index // H
        head_idx = flat_index % H
        kv_head = head_idx // group_len
        query_seq = lax.dynamic_index_in_dim(queries, batch_idx, 0, False)
        key_seq = lax.dynamic_index_in_dim(keys, batch_idx, 0, False)
        value_seq = lax.dynamic_index_in_dim(values, batch_idx, 0, False)
        query_rows = lax.dynamic_slice_in_dim(query_seq, (head_idx * HD).astype(jnp.int32), HD, 1)
        key_rows = lax.dynamic_slice_in_dim(key_seq, (kv_head * HD).astype(jnp.int32), HD, 1)
        value_rows = lax.dynamic_slice_in_dim(value_seq, (kv_head * HD).astype(jnp.int32), HD, 1)
        return attend_head(query_rows, key_rows, value_rows)

    stacked = lax.map(one_head, jnp.arange(BATCH * H, dtype=jnp.int32))
    return stacked.reshape(BATCH, H, SEQ, HD).transpose(0, 2, 1, 3).reshape(BATCH, SEQ, H * HD)


def expert_rows(token_rows, grad_rows, gate_proj, up_proj, down_proj):
    hgate = jnp.dot(token_rows, gate_proj, preferred_element_type=jnp.float32)
    hup = jnp.dot(token_rows, up_proj, preferred_element_type=jnp.float32)
    sigmoid_gate = jax.nn.sigmoid(hgate)
    silu_gate = hgate * sigmoid_gate
    activated = (silu_gate * hup).astype(jnp.bfloat16)
    expert_out = jnp.dot(activated, down_proj, preferred_element_type=jnp.float32).astype(jnp.bfloat16)
    grad_act = lax.dot_general(grad_rows, down_proj, (((1,), (1,)), ((), ())), preferred_element_type=jnp.float32)
    grad_gate = (grad_act * hup * sigmoid_gate * (1.0 + hgate * (1.0 - sigmoid_gate))).astype(jnp.bfloat16)
    grad_up = (grad_act * silu_gate).astype(jnp.bfloat16)
    input_grad = lax.dot_general(grad_gate, gate_proj, (((1,), (1,)), ((), ())), preferred_element_type=jnp.float32)
    input_grad = input_grad + lax.dot_general(grad_up, up_proj, (((1,), (1,)), ((), ())), preferred_element_type=jnp.float32)
    return expert_out, input_grad.astype(jnp.bfloat16)


def experts_layer(moe_x, expert_ids, gates, grad_out, w_gate, w_up, w_down):
    devices = N_SEQ * N_TP
    slots = devices * CAP

    def one_batch(batch_idx):
        token_x = lax.dynamic_index_in_dim(moe_x, batch_idx, 0, False)
        route_ids = lax.dynamic_index_in_dim(expert_ids, batch_idx, 0, False)
        route_gates = lax.dynamic_index_in_dim(gates, batch_idx, 0, False)
        token_grad = lax.dynamic_index_in_dim(grad_out, batch_idx, 0, False)
        owner_ids = route_ids.reshape(devices, MOE_TOK * TOPK)
        onehot = (owner_ids[:, :, None] == jnp.arange(EXPERTS, dtype=jnp.int32)[None, None, :]).astype(jnp.int32)
        before = jnp.cumsum(onehot, axis=1) - onehot
        rank_in = jnp.sum(before * onehot, axis=2)
        device_ids = jnp.arange(devices, dtype=jnp.int32)[:, None]
        slot_place = (owner_ids * slots + device_ids * CAP + rank_in).reshape(-1).astype(jnp.int32)
        token_ids = (jnp.arange(devices * MOE_TOK * TOPK, dtype=jnp.int32) // TOPK).astype(jnp.int32)
        token_table = jnp.zeros((EXPERTS * slots,), jnp.int32).at[slot_place].set(token_ids)
        gate_table = jnp.zeros((EXPERTS * slots,), jnp.float32).at[slot_place].set(route_gates.reshape(-1))
        live_table = jnp.zeros((EXPERTS * slots,), jnp.float32).at[slot_place].set(1.0)
        token_table = token_table.reshape(EXPERTS, slots)
        gate_table = gate_table.reshape(EXPERTS, slots)
        live_table = live_table.reshape(EXPERTS, slots)

        def one_expert(expert_idx):
            slot_tokens = token_table[expert_idx]
            token_rows = jnp.where(live_table[expert_idx][:, None] > 0, token_x[slot_tokens], jnp.zeros((), jnp.bfloat16))
            grad_rows = (gate_table[expert_idx][:, None] * token_grad[slot_tokens].astype(jnp.float32)).astype(jnp.bfloat16)
            return expert_rows(token_rows, grad_rows, w_gate[expert_idx], w_up[expert_idx], w_down[expert_idx])

        outs_all, grads_all = lax.map(one_expert, jnp.arange(EXPERTS, dtype=jnp.int32))
        flat_tokens = token_table.reshape(-1)
        mixed = jnp.zeros((GROUP_TOK, D), jnp.float32).at[flat_tokens].add(gate_table.reshape(-1)[:, None] * outs_all.reshape(-1, D).astype(jnp.float32))
        summed = jnp.zeros((GROUP_TOK, D), jnp.float32).at[flat_tokens].add(live_table.reshape(-1)[:, None] * grads_all.reshape(-1, D).astype(jnp.float32))
        return mixed.astype(jnp.bfloat16), summed.astype(jnp.bfloat16)

    return lax.map(one_batch, jnp.arange(N_GROUP, dtype=jnp.int32))


def reference(queries, keys, values, moe_x, expert_ids, gates, grad_out, w_gate, w_up, w_down):
    attn_out = attention(queries, keys, values)
    moe_out, moe_grad_in = experts_layer(moe_x, expert_ids, gates, grad_out, w_gate, w_up, w_down)
    return (attn_out, moe_out, moe_grad_in)
```

```python
import functools

import jax
import jax.numpy as jnp
from jax import lax
from jax.experimental import pallas as pl
from jax.experimental.pallas import tpu as pltpu
from jax.sharding import PartitionSpec as P

H = 32
KVH = 4
HD = 128
CAP = 3
LINE = 8
CHUNK = 4
MESH = pl.DeviceIdType.MESH
NT_DIMS = (((1,), (1,)), ((), ()))
F32 = jnp.float32
BF16 = jnp.bfloat16
NEG = -1e30


def fused(
    cfg,
    x_ref,
    ids_ref,
    gates_ref,
    grad_ref,
    k_ref,
    v_ref,
    q_hbm,
    wg_hbm,
    wu_hbm,
    wd_hbm,
    attn_hbm,
    mo_ref,
    mg_ref,
    wg,
    wu,
    wd,
    qbuf,
    kbuf,
    vbuf,
    obuf,
    m_s,
    l_s,
    acc_s,
    meta,
    metag,
    xg,
    gg,
    sel_s,
    selg_s,
    sx,
    sg,
    rx,
    rg,
    so,
    si,
    bo,
    bi,
    po_s,
    pi_s,
    po,
    pi,
    line_send,
    line_recv,
    kv_send,
    kv_recv,
    pair_send,
    pair_recv,
    local_sem,
):
    n_group, line, tok, topk, chunk = cfg
    chips = n_group // 2
    rows = line * CAP * line
    part = CAP * line
    width = x_ref.shape[1]
    g = lax.axis_index("group")
    seq = lax.axis_index("seq")
    tp = lax.axis_index("tp")
    core = lax.rem(g, 2)
    chip = g // 2
    y = lax.rem(seq, line)
    z = (seq // line) * 2 + tp
    a = z + core * (y - z)
    b = y + core * (z - y)

    def peer(aa, bb):
        yy = bb + core * (aa - bb)
        zz = aa + core * (bb - aa)
        return (g, (zz // 2) * line + yy, lax.rem(zz, 2))

    def in_group(j):
        return (j, seq, tp)

    other = 1 - core
    sibling = in_group(2 * chip + other)

    loads = [
        pltpu.make_async_copy(wg_hbm, wg, local_sem.at[0]),
        pltpu.make_async_copy(wu_hbm, wu, local_sem.at[1]),
        pltpu.make_async_copy(wd_hbm, wd, local_sem.at[2]),
    ]
    for load in loads:
        load.start()
    half = qbuf.shape[2]
    mine = pl.ds(pl.multiple_of(core * half, half), half)
    theirs = pl.ds(pl.multiple_of(other * half, half), half)
    q_load = pltpu.make_async_copy(q_hbm.at[:, mine], qbuf.at[core], local_sem.at[3])
    q_load.start()

    barrier = pltpu.get_barrier_semaphore()

    def greet_line(i, carry):
        pl.semaphore_signal(barrier, 1, device_id=peer(lax.rem(a + i, line), b), device_id_type=MESH)
        pl.semaphore_signal(barrier, 1, device_id=peer(a, lax.rem(b + i, line)), device_id_type=MESH)
        return carry

    lax.fori_loop(1, line, greet_line, 0)

    def greet_group(i, carry):
        pl.semaphore_signal(
            barrier, 1, device_id=in_group(lax.rem(g + i, n_group)), device_id_type=MESH
        )
        return carry

    lax.fori_loop(1, n_group, greet_group, 0)

    meta[...] = jnp.zeros_like(meta)
    meta[0:tok, 0:topk] = ids_ref[...].astype(F32)
    meta[tok : 2 * tok, 0:topk] = gates_ref[...]
    metag[a] = meta[...]
    xg[a] = x_ref[...]
    gg[a] = grad_ref[...]
    head_k = pl.ds(pl.multiple_of(core * HD, HD), HD)
    kbuf[g] = k_ref[:, head_k]
    vbuf[g] = v_ref[:, head_k]

    @pl.when(lax.rem(chip, 2) == 0)
    def _():
        for extra in (2, 3):
            kbuf[2 * chip + extra] = jnp.zeros(kbuf.shape[1:], BF16)
            vbuf[2 * chip + extra] = jnp.zeros(vbuf.shape[1:], BF16)

    pl.semaphore_wait(barrier, 2 * (line - 1) + n_group - 1)

    def along_a(f, source, dest, i):
        p = lax.rem(a + i, line)
        return pltpu.make_async_remote_copy(
            src_ref=source(p),
            dst_ref=dest.at[a],
            send_sem=line_send.at[f, i],
            recv_sem=line_recv.at[f, a],
            device_id=peer(p, b),
            device_id_type=MESH,
        )

    def along_b(f, source, dest, i):
        p = lax.rem(b + i, line)
        return pltpu.make_async_remote_copy(
            src_ref=source(p),
            dst_ref=dest.at[b],
            send_sem=line_send.at[f, i],
            recv_sem=line_recv.at[f, b],
            device_id=peer(a, p),
            device_id_type=MESH,
        )

    def send_all(copy, f, source, dest):
        def step(i, carry):
            copy(f, source, dest, i).start()
            return carry

        lax.fori_loop(1, line, step, 0)

    def sent_all(copy, f, source, dest):
        def step(i, carry):
            copy(f, source, dest, i).wait_send()
            return carry

        lax.fori_loop(1, line, step, 0)

    def wait_all(f, me, dest):
        def step(i, carry):
            p = lax.rem(me + i, line)
            pltpu.make_async_remote_copy(
                src_ref=dest.at[p],
                dst_ref=dest.at[p],
                send_sem=line_send.at[f, i],
                recv_sem=line_recv.at[f, p],
                device_id=peer(a, b),
                device_id_type=MESH,
            ).wait_recv()
            return carry

        lax.fori_loop(1, line, step, 0)

    send_all(along_a, 0, lambda p: meta, metag)
    send_all(along_a, 1, lambda p: x_ref, xg)

    def kv_copy(j, what, source, dest):
        cols = pl.ds(pl.multiple_of(lax.rem(j, 2) * HD, HD), HD)
        return pltpu.make_async_remote_copy(
            src_ref=source.at[:, cols],
            dst_ref=dest.at[g],
            send_sem=kv_send.at[what, j],
            recv_sem=kv_recv.at[what, g],
            device_id=in_group(j),
            device_id_type=MESH,
        )

    def kv_start(j, carry):
        @pl.when(j != g)
        def _():
            kv_copy(j, 0, k_ref, kbuf).start()
            kv_copy(j, 1, v_ref, vbuf).start()

        return carry

    lax.fori_loop(2 * chip, n_group, kv_start, 0)
    q_send = pltpu.make_async_remote_copy(
        src_ref=q_hbm.at[:, theirs],
        dst_ref=qbuf.at[core],
        send_sem=pair_send.at[0],
        recv_sem=pair_recv.at[0],
        device_id=sibling,
        device_id_type=MESH,
    )
    q_send.start()
    send_all(along_a, 2, lambda p: grad_ref, gg)

    wait_all(0, a, metag)
    n_tok = line * tok
    lanes = meta.shape[1]
    ids_t = metag[:, 0:tok, :].reshape(n_tok, lanes).T[0:topk]
    gates_t = metag[:, tok : 2 * tok, :].reshape(n_tok, lanes).T[0:topk]
    place = lax.broadcasted_iota(jnp.int32, (line, n_tok), 0)
    first = ((a // 2) * line + place) * 2 + lax.rem(a, 2)
    second = ((place // 2) * line + a) * 2 + lax.rem(place, 2)
    expert = (first + core * (second - first)).astype(F32)
    named = jnp.zeros((line, n_tok), F32)
    gate = jnp.zeros((line, n_tok), F32)
    for k in range(topk):
        hit = jnp.where(ids_t[k : k + 1] == expert, 1.0, 0.0)
        named = named + hit
        gate = gate + hit * gates_t[k : k + 1]
    t_row = lax.broadcasted_iota(jnp.int32, (n_tok, n_tok), 0)
    t_col = lax.broadcasted_iota(jnp.int32, (n_tok, n_tok), 1)
    earlier = jnp.where((t_row // tok == t_col // tok) & (t_row < t_col), 1.0, 0.0)
    rank = jnp.dot(named.astype(BF16), earlier.astype(BF16), preferred_element_type=F32)
    own_block = jnp.where(place == lax.broadcasted_iota(jnp.int32, (line, n_tok), 1) // tok, 1.0, 0.0)
    for s in range(CAP):
        slot = jnp.where(rank == s, named, 0.0)
        slot_gate = slot * gate
        for d in range(line):
            at = pl.ds(d * part + s * line, line)
            sel_s[at] = own_block * slot[d : d + 1]
            selg_s[at] = own_block * slot_gate[d : d + 1]
    sel = sel_s[...]
    sel_b = sel.astype(BF16)
    gate_col = jnp.sum(selg_s[...], axis=1, keepdims=True)

    tile = min(width, 512)

    def rows_of(ref, cols):
        return jnp.concatenate(
            [ref[d, s, :, cols].astype(F32) for d in range(line) for s in range(CAP)], axis=0
        ).astype(BF16)

    def put_rows(ref, cols, value):
        for d in range(line):
            for s in range(CAP):
                r = d * part + s * line
                ref[d, s, :, cols] = value[r : r + line].astype(BF16)

    def pick(source, dest, received, scale):
        for c in range(0, width, tile):
            cols = slice(c, c + tile)
            block = source[:, :, cols].reshape(n_tok, tile)
            picked = jnp.dot(sel_b, block, preferred_element_type=F32)
            if scale is not None:
                picked = picked * scale
            put_rows(dest, cols, picked)
        received[b] = dest[b]

    wait_all(1, a, xg)
    pick(xg, sx, rx, None)
    send_all(along_b, 3, lambda p: sx.at[p], rx)
    wait_all(2, a, gg)
    pick(gg, sg, rg, gate_col)
    send_all(along_b, 4, lambda p: sg.at[p], rg)

    for load in loads:
        load.wait()

    wait_all(3, b, rx)
    ffe = wg.shape[1]
    hgate = jnp.zeros((rows, ffe), F32)
    hup = jnp.zeros((rows, ffe), F32)
    for c in range(0, width, tile):
        cols = slice(c, c + tile)
        token_rows = rows_of(rx, cols)
        hgate = hgate + jnp.dot(token_rows, wg[cols, :], preferred_element_type=F32)
        hup = hup + jnp.dot(token_rows, wu[cols, :], preferred_element_type=F32)
    sig = 1.0 / (1.0 + jnp.exp(-hgate))
    silu = hgate * sig
    act = (silu * hup).astype(BF16)
    for c in range(0, width, tile):
        cols = slice(c, c + tile)
        put_rows(so, cols, jnp.dot(act, wd[:, cols], preferred_element_type=F32))
    bo[b] = so[b]
    send_all(along_b, 5, lambda p: so.at[p], bo)

    wait_all(4, b, rg)
    grad_act = jnp.zeros((rows, ffe), F32)
    for c in range(0, width, tile):
        cols = slice(c, c + tile)
        grad_act = grad_act + lax.dot_general(
            rows_of(rg, cols), wd[:, cols], NT_DIMS, preferred_element_type=F32
        )
    grad_gate = (grad_act * hup * sig * (1.0 + hgate * (1.0 - sig))).astype(BF16)
    grad_up = (grad_act * silu).astype(BF16)
    for c in range(0, width, tile):
        cols = slice(c, c + tile)
        put_rows(
            si,
            cols,
            lax.dot_general(grad_gate, wg[cols, :], NT_DIMS, preferred_element_type=F32)
            + lax.dot_general(grad_up, wu[cols, :], NT_DIMS, preferred_element_type=F32),
        )
    bi[b] = si[b]
    send_all(along_b, 6, lambda p: si.at[p], bi)

    q_load.wait()
    q_send.wait_recv()

    def kv_wait(j, carry):
        @pl.when(j != g)
        def _():
            for what, dest in ((0, kbuf), (1, vbuf)):
                pltpu.make_async_remote_copy(
                    src_ref=dest.at[j],
                    dst_ref=dest.at[j],
                    send_sem=kv_send.at[what, j],
                    recv_sem=kv_recv.at[what, j],
                    device_id=sibling,
                    device_id_type=MESH,
                ).wait_recv()

        return carry

    lax.fori_loop(0, 2 * chip + 2, kv_wait, 0)
    n_heads = half // HD
    pos = k_ref.shape[0]
    q_rows = 2 * pos
    keys = chunk * pos
    m_s[...] = jnp.full_like(m_s, NEG)
    l_s[...] = jnp.zeros_like(l_s)
    acc_s[...] = jnp.zeros_like(acc_s)
    exp_scale = 1.4426950408889634 / HD**0.5

    def attend(j, carry):
        key_rows = kbuf[pl.ds(j * chunk, chunk)].reshape(keys, HD)
        value_rows = vbuf[pl.ds(j * chunk, chunk)].reshape(keys, HD)
        ahead = lax.broadcasted_iota(jnp.int32, (q_rows, keys), 1) - lax.broadcasted_iota(
            jnp.int32, (q_rows, keys), 0
        )
        seen = ahead <= q_rows * chip - keys * j
        for h in range(n_heads):
            cols = slice(h * HD, (h + 1) * HD)
            query_rows = qbuf[:, :, cols].reshape(q_rows, HD)
            scores = lax.dot_general(query_rows, key_rows, NT_DIMS, preferred_element_type=F32)
            scores = jnp.where(seen, scores, NEG)
            m_old = m_s[h]
            m_new = jnp.maximum(m_old, jnp.max(scores, axis=1, keepdims=True))
            alpha = jnp.exp2((m_old - m_new) * exp_scale)
            total = alpha * l_s[h]
            weights = []
            for c in range(0, keys, HD):
                e = jnp.exp2((scores[:, c : c + HD] - m_new) * exp_scale)
                total = total + e
                weights.append(e.astype(BF16))
            m_s[h] = m_new
            l_s[h] = total
            acc_s[h] = alpha * acc_s[h] + jnp.dot(
                jnp.concatenate(weights, axis=1), value_rows, preferred_element_type=F32
            )
        return carry

    lax.fori_loop(0, (2 * chip + 1 + chunk) // chunk, attend, 0)
    for h in range(n_heads):
        cols = slice(h * HD, (h + 1) * HD)
        done = acc_s[h] / jnp.sum(l_s[h], axis=1, keepdims=True)
        obuf[:, :, cols] = done.astype(BF16).reshape(2, pos, HD)
    o_send = pltpu.make_async_remote_copy(
        src_ref=obuf.at[other],
        dst_ref=attn_hbm.at[:, mine],
        send_sem=pair_send.at[1],
        recv_sem=pair_recv.at[1],
        device_id=sibling,
        device_id_type=MESH,
    )
    o_send.start()
    o_store = pltpu.make_async_copy(obuf.at[core], attn_hbm.at[:, mine], local_sem.at[3])
    o_store.start()

    gated_hi = selg_s[...].astype(BF16)
    gated_lo = (selg_s[...] - gated_hi.astype(F32)).astype(BF16)
    hi_t = gated_hi.astype(F32).T.astype(BF16)
    lo_t = gated_lo.astype(F32).T.astype(BF16)
    sel_t = sel.T.astype(BF16)

    def mix(returned, dest, final, lefts):
        for c in range(0, width, tile):
            cols = slice(c, c + tile)
            block = rows_of(returned, cols)
            mixed = jnp.dot(lefts[0], block, preferred_element_type=F32)
            for left in lefts[1:]:
                mixed = mixed + jnp.dot(left, block, preferred_element_type=F32)
            dest[:, :, cols] = mixed.astype(BF16).reshape(line, tok, tile)
        final[a] = dest[a]

    wait_all(5, b, bo)
    mix(bo, po_s, po, (hi_t, lo_t))
    send_all(along_a, 7, lambda p: po_s.at[p], po)
    wait_all(6, b, bi)
    mix(bi, pi_s, pi, (sel_t,))
    send_all(along_a, 8, lambda p: pi_s.at[p], pi)

    def add_up(final, out):
        total = final[0].astype(F32)
        for p in range(1, line):
            total = total + final[p].astype(F32)
        out[...] = total.astype(BF16)

    wait_all(7, a, po)
    add_up(po, mo_ref)
    wait_all(8, a, pi)
    add_up(pi, mg_ref)

    o_store.wait()
    o_send.wait()
    q_send.wait_send()
    sent_all(along_a, 0, lambda p: meta, metag)
    sent_all(along_a, 1, lambda p: x_ref, xg)
    sent_all(along_a, 2, lambda p: grad_ref, gg)
    sent_all(along_b, 3, lambda p: sx.at[p], rx)
    sent_all(along_b, 4, lambda p: sg.at[p], rg)
    sent_all(along_b, 5, lambda p: so.at[p], bo)
    sent_all(along_b, 6, lambda p: si.at[p], bi)
    sent_all(along_a, 7, lambda p: po_s.at[p], po)
    sent_all(along_a, 8, lambda p: pi_s.at[p], pi)

    def kv_sent(j, carry):
        @pl.when(j != g)
        def _():
            kv_copy(j, 0, k_ref, kbuf).wait_send()
            kv_copy(j, 1, v_ref, vbuf).wait_send()

        return carry

    lax.fori_loop(2 * chip, n_group, kv_sent, 0)


def shards(queries, keys, values, moe_x, expert_ids, gates, grad_out, w_gate, w_up, w_down):
    n_group = lax.axis_size("group")
    line = LINE
    pos, q_width = queries.shape[1:]
    tok, width = moe_x.shape[1:]
    topk = expert_ids.shape[2]
    ffe = w_gate.shape[2]
    half = q_width // 2
    n_heads = half // HD
    rows = line * CAP * line
    n_tok = line * tok
    chunk = min(CHUNK, n_group)
    vmem = pl.BlockSpec(memory_space=pltpu.VMEM)
    hbm = pl.BlockSpec(memory_space=pl.ANY)
    slots = pltpu.VMEM((line, CAP, line, width), BF16)
    block = pltpu.VMEM((line, tok, width), BF16)
    state = pltpu.VMEM((n_heads, 2 * pos, HD), F32)
    attn, out, grad_in = pl.pallas_call(
        functools.partial(fused, (n_group, line, tok, topk, chunk)),
        out_shape=(
            jax.ShapeDtypeStruct((pos, q_width), BF16),
            jax.ShapeDtypeStruct((tok, width), BF16),
            jax.ShapeDtypeStruct((tok, width), BF16),
        ),
        in_specs=[vmem] * 6 + [hbm] * 4,
        out_specs=(hbm, vmem, vmem),
        scratch_shapes=[
            pltpu.VMEM((width, ffe), BF16),
            pltpu.VMEM((width, ffe), BF16),
            pltpu.VMEM((ffe, width), BF16),
            pltpu.VMEM((2, pos, half), BF16),
            pltpu.VMEM((n_group, pos, HD), BF16),
            pltpu.VMEM((n_group, pos, HD), BF16),
            pltpu.VMEM((2, pos, half), BF16),
            state,
            state,
            state,
            pltpu.VMEM((2 * tok, 128), F32),
            pltpu.VMEM((line, 2 * tok, 128), F32),
            block,
            block,
            pltpu.VMEM((rows, n_tok), F32),
            pltpu.VMEM((rows, n_tok), F32),
        ]
        + [slots] * 8
        + [block] * 4
        + [
            pltpu.SemaphoreType.DMA((9, line)),
            pltpu.SemaphoreType.DMA((9, line)),
            pltpu.SemaphoreType.DMA((2, n_group)),
            pltpu.SemaphoreType.DMA((2, n_group)),
            pltpu.SemaphoreType.DMA((2,)),
            pltpu.SemaphoreType.DMA((2,)),
            pltpu.SemaphoreType.DMA((4,)),
        ],
        compiler_params=pltpu.CompilerParams(
            collective_id=0, has_side_effects=True, vmem_limit_bytes=60 * 1024 * 1024
        ),
    )(
        moe_x[0],
        expert_ids[0],
        gates[0],
        grad_out[0],
        keys[0],
        values[0],
        queries[0],
        w_gate[0],
        w_up[0],
        w_down[0],
    )
    return attn[None], out[None], grad_in[None]


def solution(mesh):
    tokens = P("group", ("seq", "tp"), None)
    heads = P("seq", "group", "tp")
    weights = P(("seq", "tp"), None, None)
    return jax.shard_map(
        shards,
        mesh=mesh,
        in_specs=(heads,) * 3 + (tokens,) * 4 + (weights,) * 3,
        out_specs=(heads, tokens, tokens),
        check_vma=False,
    )
```

```python
import functools

import jax
import jax.numpy as jnp
from jax import lax
from jax.experimental import pallas as pl
from jax.experimental.pallas import tpu as pltpu
from jax.sharding import PartitionSpec as P

H = 32
KVH = 4
HD = 128
CAP = 3
LINE = 8
CHUNK = 4
MESH = pl.DeviceIdType.MESH
NT_DIMS = (((1,), (1,)), ((), ()))
F32 = jnp.float32
BF16 = jnp.bfloat16
NEG = -1e30


def fused(
    cfg,
    x_hbm,
    ids_hbm,
    gates_hbm,
    grad_hbm,
    k_hbm,
    v_hbm,
    q_hbm,
    wg_hbm,
    wu_hbm,
    wd_hbm,
    attn_hbm,
    mo_ref,
    mg_ref,
    wg,
    wu,
    wd,
    qbuf,
    kbuf,
    vbuf,
    obuf,
    m_s,
    l_s,
    acc_s,
    idsg,
    gatesg,
    xg,
    gg,
    sel_s,
    selg_s,
    sx,
    sg,
    rx,
    rg,
    so,
    si,
    bo,
    bi,
    po_s,
    pi_s,
    po_r,
    pi,
    line_send,
    line_recv,
    kv_send,
    kv_recv,
    pair_send,
    pair_recv,
    local_sem,
):
    n_group, line, tok, topk, chunk = cfg
    chips = n_group // 2
    rows = line * CAP * line
    part = CAP * line
    width = x_hbm.shape[1]
    g = lax.axis_index("group")
    seq = lax.axis_index("seq")
    tp = lax.axis_index("tp")
    core = lax.rem(g, 2)
    chip = g // 2
    y = lax.rem(seq, line)
    z = (seq // line) * 2 + tp
    a = z + core * (y - z)
    b = y + core * (z - y)

    def peer(aa, bb):
        yy = bb + core * (aa - bb)
        zz = aa + core * (bb - aa)
        return (g, (zz // 2) * line + yy, lax.rem(zz, 2))

    def in_group(j):
        return (j, seq, tp)

    other = 1 - core
    sibling = in_group(2 * chip + other)

    barrier = pltpu.get_barrier_semaphore()

    def greet_line(i, carry):
        pl.semaphore_signal(barrier, 1, device_id=peer(lax.rem(a + i, line), b), device_id_type=MESH)
        pl.semaphore_signal(barrier, 1, device_id=peer(a, lax.rem(b + i, line)), device_id_type=MESH)
        return carry

    lax.fori_loop(1, line, greet_line, 0)

    def greet_group(i, carry):
        pl.semaphore_signal(
            barrier, 1, device_id=in_group(lax.rem(g + i, n_group)), device_id_type=MESH
        )
        return carry

    lax.fori_loop(1, n_group, greet_group, 0)

    half = qbuf.shape[2]
    mine = pl.ds(pl.multiple_of(core * half, half), half)
    theirs = pl.ds(pl.multiple_of(other * half, half), half)
    head = pl.ds(pl.multiple_of(core * HD, HD), HD)
    early = [
        pltpu.make_async_copy(ids_hbm, idsg.at[a], local_sem.at[0]),
        pltpu.make_async_copy(gates_hbm, gatesg.at[a], local_sem.at[1]),
        pltpu.make_async_copy(x_hbm, xg.at[a], local_sem.at[2]),
        pltpu.make_async_copy(grad_hbm, gg.at[a], local_sem.at[3]),
    ]
    own_heads = [
        pltpu.make_async_copy(q_hbm.at[:, mine], qbuf.at[core], local_sem.at[4]),
        pltpu.make_async_copy(k_hbm.at[:, head], kbuf.at[g], local_sem.at[5]),
        pltpu.make_async_copy(v_hbm.at[:, head], vbuf.at[g], local_sem.at[6]),
    ]
    loads = [
        pltpu.make_async_copy(wg_hbm, wg, local_sem.at[7]),
        pltpu.make_async_copy(wu_hbm, wu, local_sem.at[8]),
        pltpu.make_async_copy(wd_hbm, wd, local_sem.at[9]),
    ]
    for load in early + own_heads + loads:
        load.start()

    @pl.when((lax.rem(chip, 2) == 0) & (chunk > 2))
    def _():
        for extra in range(2, chunk):
            kbuf[2 * chip + extra] = jnp.zeros(kbuf.shape[1:], BF16)
            vbuf[2 * chip + extra] = jnp.zeros(vbuf.shape[1:], BF16)

    pl.semaphore_wait(barrier, 2 * (line - 1) + n_group - 1)

    def distance(i):
        odd = lax.rem(i, 2)
        return odd * ((i + 1) // 2) + (1 - odd) * (line - i // 2)

    def along_a(f, source, dest, i):
        p = lax.rem(a + distance(i), line)
        return pltpu.make_async_remote_copy(
            src_ref=source(p),
            dst_ref=dest.at[a],
            send_sem=line_send.at[f, i],
            recv_sem=line_recv.at[f, a],
            device_id=peer(p, b),
            device_id_type=MESH,
        )

    def along_b(f, source, dest, i):
        p = lax.rem(b + distance(i), line)
        return pltpu.make_async_remote_copy(
            src_ref=source(p),
            dst_ref=dest.at[b],
            send_sem=line_send.at[f, i],
            recv_sem=line_recv.at[f, b],
            device_id=peer(a, p),
            device_id_type=MESH,
        )

    def send_all(copy, f, source, dest):
        def step(i, carry):
            copy(f, source, dest, i).start()
            return carry

        lax.fori_loop(1, line, step, 0)

    def sent_all(copy, f, source, dest):
        def step(i, carry):
            copy(f, source, dest, i).wait_send()
            return carry

        lax.fori_loop(1, line, step, 0)

    def wait_all(f, me, dest):
        def step(i, carry):
            p = lax.rem(me + i, line)
            pltpu.make_async_remote_copy(
                src_ref=dest.at[p],
                dst_ref=dest.at[p],
                send_sem=line_send.at[f, i],
                recv_sem=line_recv.at[f, p],
                device_id=peer(a, b),
                device_id_type=MESH,
            ).wait_recv()
            return carry

        lax.fori_loop(1, line, step, 0)

    send_all(along_a, 0, lambda p: ids_hbm, idsg)
    send_all(along_a, 9, lambda p: gates_hbm, gatesg)
    send_all(along_a, 1, lambda p: x_hbm, xg)

    n_up = line // 2
    n_down = line - 1 - n_up
    above = peer(lax.rem(a + 1, line), b)
    below = peer(lax.rem(a + line - 1, line), b)

    def ring_copy(f, up, step, source, dest):
        n = step if up else n_up + step
        return pltpu.make_async_remote_copy(
            src_ref=source,
            dst_ref=dest,
            send_sem=line_send.at[f, n],
            recv_sem=line_recv.at[f, n],
            device_id=above if up else below,
            device_id_type=MESH,
        )

    def gather_step(up, step):
        p = lax.rem(a - step + line if up else a + step, line)
        return ring_copy(2, up, step, grad_hbm if step == 0 else gg.at[p], gg.at[p])

    def gather_send(step):
        for up, n in ((True, n_up), (False, n_down)):
            if step < n:
                if step > 0:
                    gather_step(up, step - 1).wait_recv()
                gather_step(up, step).start()

    gather_send(0)

    def kv_copy(j, what, source, dest):
        cols = pl.ds(pl.multiple_of(lax.rem(j, 2) * HD, HD), HD)
        return pltpu.make_async_remote_copy(
            src_ref=source.at[:, cols],
            dst_ref=dest.at[g],
            send_sem=kv_send.at[what, j],
            recv_sem=kv_recv.at[what, g],
            device_id=in_group(j),
            device_id_type=MESH,
        )

    def kv_start(j, carry):
        @pl.when(j != g)
        def _():
            kv_copy(j, 0, k_hbm, kbuf).start()
            kv_copy(j, 1, v_hbm, vbuf).start()

        return carry

    lax.fori_loop(2 * chip, n_group, kv_start, 0)
    q_send = pltpu.make_async_remote_copy(
        src_ref=q_hbm.at[:, theirs],
        dst_ref=qbuf.at[core],
        send_sem=pair_send.at[0],
        recv_sem=pair_recv.at[0],
        device_id=sibling,
        device_id_type=MESH,
    )
    q_send.start()
    for load in early:
        load.wait()

    wait_all(0, a, idsg)
    wait_all(9, a, gatesg)
    n_tok = line * tok
    ids_t = jnp.concatenate([idsg[p] for p in range(line)], axis=1).astype(F32)
    gates_t = jnp.concatenate([gatesg[p] for p in range(line)], axis=1)
    place = lax.broadcasted_iota(jnp.int32, (line, n_tok), 0)
    first = ((a // 2) * line + place) * 2 + lax.rem(a, 2)
    second = ((place // 2) * line + a) * 2 + lax.rem(place, 2)
    expert = (first + core * (second - first)).astype(F32)
    named = jnp.zeros((line, n_tok), F32)
    gate = jnp.zeros((line, n_tok), F32)
    for k in range(topk):
        hit = jnp.where(ids_t[k : k + 1] == expert, 1.0, 0.0)
        named = named + hit
        gate = gate + hit * gates_t[k : k + 1]
    t_row = lax.broadcasted_iota(jnp.int32, (n_tok, n_tok), 0)
    t_col = lax.broadcasted_iota(jnp.int32, (n_tok, n_tok), 1)
    earlier = jnp.where((t_row // tok == t_col // tok) & (t_row < t_col), 1.0, 0.0)
    rank = jnp.dot(named.astype(BF16), earlier.astype(BF16), preferred_element_type=F32)
    own_block = jnp.where(place == lax.broadcasted_iota(jnp.int32, (line, n_tok), 1) // tok, 1.0, 0.0)
    for s in range(CAP):
        slot = jnp.where(rank == s, named, 0.0)
        slot_gate = slot * gate
        for d in range(line):
            at = pl.ds(d * part + s * line, line)
            sel_s[at] = own_block * slot[d : d + 1]
            selg_s[at] = own_block * slot_gate[d : d + 1]
    sel = sel_s[...]
    sel_b = sel.astype(BF16)
    gate_col = jnp.sum(selg_s[...], axis=1, keepdims=True)

    tile = min(width, 512)

    def rows_of(ref, cols):
        return jnp.concatenate(
            [ref[d, s, :, cols].astype(F32) for d in range(line) for s in range(CAP)], axis=0
        ).astype(BF16)

    def put_rows(ref, cols, value):
        for d in range(line):
            for s in range(CAP):
                r = d * part + s * line
                ref[d, s, :, cols] = value[r : r + line].astype(BF16)

    def pick(source, dest, received, scale):
        for c in range(0, width, tile):
            cols = slice(c, c + tile)
            block = source[:, :, cols].reshape(n_tok, tile)
            picked = jnp.dot(sel_b, block, preferred_element_type=F32)
            if scale is not None:
                picked = picked * scale
            put_rows(dest, cols, picked)
        received[b] = dest[b]

    for step in range(1, n_up - 1):
        gather_send(step)
    wait_all(1, a, xg)
    pick(xg, sx, rx, None)
    send_all(along_b, 3, lambda p: sx.at[p], rx)
    if n_up > 1:
        gather_send(n_up - 1)
    gather_step(True, n_up - 1).wait_recv()
    if n_down > 0:
        gather_step(False, n_down - 1).wait_recv()
    pick(gg, sg, rg, gate_col)
    send_all(along_b, 4, lambda p: sg.at[p], rg)

    for load in loads:
        load.wait()

    wait_all(3, b, rx)
    ffe = wg.shape[1]
    hgate = jnp.zeros((rows, ffe), F32)
    hup = jnp.zeros((rows, ffe), F32)
    for c in range(0, width, tile):
        cols = slice(c, c + tile)
        token_rows = rows_of(rx, cols)
        hgate = hgate + jnp.dot(token_rows, wg[cols, :], preferred_element_type=F32)
        hup = hup + jnp.dot(token_rows, wu[cols, :], preferred_element_type=F32)
    sig = 1.0 / (1.0 + jnp.exp(-hgate))
    silu = hgate * sig
    act = (silu * hup).astype(BF16)
    for c in range(0, width, tile):
        cols = slice(c, c + tile)
        put_rows(so, cols, jnp.dot(act, wd[:, cols], preferred_element_type=F32))
    bo[b] = so[b]
    send_all(along_b, 5, lambda p: so.at[p], bo)

    n_heads = half // HD
    pos = k_hbm.shape[0]
    q_rows = 2 * pos
    keys = chunk * pos
    exp_scale = 1.4426950408889634 / HD**0.5
    n_chunks = (2 * chip + 1 + chunk) // chunk

    def kv_wait(j):
        @pl.when((j != g) & (j < 2 * chip + 2))
        def _():
            for what, dest in ((0, kbuf), (1, vbuf)):
                pltpu.make_async_remote_copy(
                    src_ref=dest.at[j],
                    dst_ref=dest.at[j],
                    send_sem=kv_send.at[what, j],
                    recv_sem=kv_recv.at[what, j],
                    device_id=sibling,
                    device_id_type=MESH,
                ).wait_recv()

    def attend(j, diagonal):
        def arrived(t, carry):
            kv_wait(j * chunk + t)
            return carry

        lax.fori_loop(0, chunk, arrived, 0)
        key_rows = kbuf[pl.ds(j * chunk, chunk)].reshape(keys, HD)
        value_rows = vbuf[pl.ds(j * chunk, chunk)].reshape(keys, HD)
        if diagonal:
            ahead = lax.broadcasted_iota(jnp.int32, (q_rows, keys), 1) - lax.broadcasted_iota(
                jnp.int32, (q_rows, keys), 0
            )
            seen = ahead <= q_rows * chip - keys * j
        for h in range(n_heads):
            cols = slice(h * HD, (h + 1) * HD)
            query_rows = qbuf[:, :, cols].reshape(q_rows, HD)
            scores = lax.dot_general(query_rows, key_rows, NT_DIMS, preferred_element_type=F32)
            if diagonal:
                scores = jnp.where(seen, scores, NEG)
            top = jnp.max(scores, axis=1, keepdims=True)
            m_new = jnp.broadcast_to(top, (q_rows, HD)) if diagonal else jnp.maximum(m_s[h], top)
            total = None
            weights = []
            for c in range(0, keys, HD):
                e = jnp.exp2((scores[:, c : c + HD] - m_new) * exp_scale)
                total = e if total is None else total + e
                weights.append(e.astype(BF16))
            mixed = jnp.dot(jnp.concatenate(weights, axis=1), value_rows, preferred_element_type=F32)
            if not diagonal:
                alpha = jnp.exp2((m_s[h] - m_new) * exp_scale)
                total = total + alpha * l_s[h]
                mixed = mixed + alpha * acc_s[h]
            m_s[h] = m_new
            l_s[h] = total
            acc_s[h] = mixed

    def attend_down(first, last):
        def step(i, carry):
            attend(n_chunks - 1 - i, False)
            return carry

        lax.fori_loop(first, last, step, 0)

    for load in own_heads:
        load.wait()
    q_send.wait_recv()
    attend(n_chunks - 1, True)
    attend_down(1, jnp.minimum(n_chunks, 2))

    wait_all(4, b, rg)
    grad_act = jnp.zeros((rows, ffe), F32)
    for c in range(0, width, tile):
        cols = slice(c, c + tile)
        grad_act = grad_act + lax.dot_general(
            rows_of(rg, cols), wd[:, cols], NT_DIMS, preferred_element_type=F32
        )
    grad_gate = (grad_act * hup * sig * (1.0 + hgate * (1.0 - sig))).astype(BF16)
    grad_up = (grad_act * silu).astype(BF16)
    for c in range(0, width, tile):
        cols = slice(c, c + tile)
        put_rows(
            si,
            cols,
            lax.dot_general(grad_gate, wg[cols, :], NT_DIMS, preferred_element_type=F32)
            + lax.dot_general(grad_up, wu[cols, :], NT_DIMS, preferred_element_type=F32),
        )
    bi[b] = si[b]
    send_all(along_b, 6, lambda p: si.at[p], bi)

    attend_down(2, n_chunks)
    for h in range(n_heads):
        cols = slice(h * HD, (h + 1) * HD)
        done = acc_s[h] / jnp.sum(l_s[h], axis=1, keepdims=True)
        obuf[:, :, cols] = done.astype(BF16).reshape(2, pos, HD)
    o_send = pltpu.make_async_remote_copy(
        src_ref=obuf.at[other],
        dst_ref=attn_hbm.at[:, mine],
        send_sem=pair_send.at[1],
        recv_sem=pair_recv.at[1],
        device_id=sibling,
        device_id_type=MESH,
    )
    o_send.start()
    o_store = pltpu.make_async_copy(obuf.at[core], attn_hbm.at[:, mine], local_sem.at[4])
    o_store.start()

    gated_hi = selg_s[...].astype(BF16)
    gated_lo = (selg_s[...] - gated_hi.astype(F32)).astype(BF16)
    hi_t = gated_hi.astype(F32).T.astype(BF16)
    lo_t = gated_lo.astype(F32).T.astype(BF16)
    sel_t = sel.T.astype(BF16)

    def mix(returned, dest, lefts):
        for c in range(0, width, tile):
            cols = slice(c, c + tile)
            block = rows_of(returned, cols)
            mixed = jnp.dot(lefts[0], block, preferred_element_type=F32)
            for left in lefts[1:]:
                mixed = mixed + jnp.dot(left, block, preferred_element_type=F32)
            dest[:, :, cols] = mixed.astype(BF16).reshape(line, tok, tile)

    wait_all(5, b, bo)
    mix(bo, po_s, (hi_t, lo_t))

    def sum_step(up, step):
        p = lax.rem(a + n_up - step if up else a + line - n_down + step, line)
        return p, ring_copy(7, up, step, po_s.at[p], po_r.at[step if up else n_up + step])

    for step in range(n_up):
        for up, n in ((True, n_up), (False, n_down)):
            if step < n:
                p, copy = sum_step(up, step)
                if step > 0:
                    sum_step(up, step - 1)[1].wait_recv()
                    got = po_r[step - 1 if up else n_up + step - 1]
                    po_s[p] = (po_s[p].astype(F32) + got.astype(F32)).astype(BF16)
                copy.start()

    wait_all(6, b, bi)
    mix(bi, pi_s, (sel_t,))
    pi[a] = pi_s[a]
    send_all(along_a, 8, lambda p: pi_s.at[p], pi)

    total = po_s[a].astype(F32)
    sum_step(True, n_up - 1)[1].wait_recv()
    total = total + po_r[n_up - 1].astype(F32)
    if n_down > 0:
        sum_step(False, n_down - 1)[1].wait_recv()
        total = total + po_r[line - 2].astype(F32)
    mo_ref[...] = total.astype(BF16)

    wait_all(8, a, pi)
    total = pi[0].astype(F32)
    for p in range(1, line):
        total = total + pi[p].astype(F32)
    mg_ref[...] = total.astype(BF16)

    o_store.wait()
    o_send.wait()
    q_send.wait_send()
    sent_all(along_a, 0, lambda p: ids_hbm, idsg)
    sent_all(along_a, 9, lambda p: gates_hbm, gatesg)
    sent_all(along_a, 1, lambda p: x_hbm, xg)
    sent_all(along_b, 3, lambda p: sx.at[p], rx)
    sent_all(along_b, 4, lambda p: sg.at[p], rg)
    sent_all(along_b, 5, lambda p: so.at[p], bo)
    sent_all(along_b, 6, lambda p: si.at[p], bi)
    for up, n in ((True, n_up), (False, n_down)):
        for step in range(n):
            gather_step(up, step).wait_send()
            sum_step(up, step)[1].wait_send()
    sent_all(along_a, 8, lambda p: pi_s.at[p], pi)

    def kv_sent(j, carry):
        @pl.when(j != g)
        def _():
            kv_copy(j, 0, k_hbm, kbuf).wait_send()
            kv_copy(j, 1, v_hbm, vbuf).wait_send()

        return carry

    lax.fori_loop(2 * chip, n_group, kv_sent, 0)


def hand_over(pieces, attn, out, grad_in, attn_o, out_o, grad_o, attn_v, out_v, grad_v, came, went):
    n = attn.shape[0] // pieces
    parts = [
        (attn.at[i * n : i * n + n], attn_v.at[i * n : i * n + n], attn_o.at[i * n : i * n + n])
        for i in range(pieces)
    ] + [(out, out_v, out_o), (grad_in, grad_v, grad_o)]
    reads = [pltpu.make_async_copy(r, v, came.at[i]) for i, (r, v, _) in enumerate(parts)]
    writes = [pltpu.make_async_copy(v, w, went.at[i]) for i, (_, v, w) in enumerate(parts)]
    for read in reads:
        read.start()
    for read, write in zip(reads, writes):
        read.wait()
        write.start()
    for write in writes:
        write.wait()


def shards(queries, keys, values, moe_x, expert_ids, gates, grad_out, w_gate, w_up, w_down):
    n_group = lax.axis_size("group")
    line = LINE
    pos, q_width = queries.shape[1:]
    tok, width = moe_x.shape[1:]
    topk = expert_ids.shape[2]
    ffe = w_gate.shape[2]
    half = q_width // 2
    n_heads = half // HD
    rows = line * CAP * line
    n_tok = line * tok
    chunk = min(CHUNK, n_group)
    vmem = pl.BlockSpec(memory_space=pltpu.VMEM)
    hbm = pl.BlockSpec(memory_space=pl.ANY)
    slots = pltpu.VMEM((line, CAP, line, width), BF16)
    block = pltpu.VMEM((line, tok, width), BF16)
    state = pltpu.VMEM((n_heads, 2 * pos, HD), F32)
    attn, out, grad_in = pl.pallas_call(
        functools.partial(fused, (n_group, line, tok, topk, chunk)),
        out_shape=(
            jax.ShapeDtypeStruct((pos, q_width), BF16),
            jax.ShapeDtypeStruct((tok, width), BF16),
            jax.ShapeDtypeStruct((tok, width), BF16),
        ),
        in_specs=[hbm] * 10,
        out_specs=(hbm, vmem, vmem),
        scratch_shapes=[
            pltpu.VMEM((width, ffe), BF16),
            pltpu.VMEM((width, ffe), BF16),
            pltpu.VMEM((ffe, width), BF16),
            pltpu.VMEM((2, pos, half), BF16),
            pltpu.VMEM((n_group, pos, HD), BF16),
            pltpu.VMEM((n_group, pos, HD), BF16),
            pltpu.VMEM((2, pos, half), BF16),
            state,
            state,
            state,
            pltpu.VMEM((line, topk, tok), jnp.int32),
            pltpu.VMEM((line, topk, tok), F32),
            block,
            block,
            pltpu.VMEM((rows, n_tok), F32),
            pltpu.VMEM((rows, n_tok), F32),
        ]
        + [slots] * 8
        + [block] * 4
        + [
            pltpu.SemaphoreType.DMA((10, line)),
            pltpu.SemaphoreType.DMA((10, line)),
            pltpu.SemaphoreType.DMA((2, n_group)),
            pltpu.SemaphoreType.DMA((2, n_group)),
            pltpu.SemaphoreType.DMA((2,)),
            pltpu.SemaphoreType.DMA((2,)),
            pltpu.SemaphoreType.DMA((10,)),
        ],
        compiler_params=pltpu.CompilerParams(
            collective_id=0, has_side_effects=True, vmem_limit_bytes=60 * 1024 * 1024
        ),
    )(
        moe_x[0],
        expert_ids[0].T,
        gates[0].T,
        grad_out[0],
        keys[0],
        values[0],
        queries[0],
        w_gate[0],
        w_up[0],
        w_down[0],
    )
    pieces = 4
    attn, out, grad_in = pl.pallas_call(
        functools.partial(hand_over, pieces),
        out_shape=tuple(jax.ShapeDtypeStruct(t.shape, BF16) for t in (attn, out, grad_in)),
        in_specs=[hbm] * 3,
        out_specs=(hbm,) * 3,
        scratch_shapes=[
            pltpu.VMEM(attn.shape, BF16),
            pltpu.VMEM(out.shape, BF16),
            pltpu.VMEM(out.shape, BF16),
            pltpu.SemaphoreType.DMA((pieces + 2,)),
            pltpu.SemaphoreType.DMA((pieces + 2,)),
        ],
    )(attn, out, grad_in)
    return attn[None], out[None], grad_in[None]


def solution(mesh):
    tokens = P("group", ("seq", "tp"), None)
    heads = P("seq", "group", "tp")
    weights = P(("seq", "tp"), None, None)
    return jax.shard_map(
        shards,
        mesh=mesh,
        in_specs=(heads,) * 3 + (tokens,) * 4 + (weights,) * 3,
        out_specs=(heads, tokens, tokens),
        check_vma=False,
    )
```

```python
import functools

import jax
import jax.numpy as jnp
from jax import lax
from jax.experimental import pallas as pl
from jax.experimental.pallas import tpu as pltpu
from jax.sharding import PartitionSpec as P

H = 32
KVH = 4
HD = 128
CAP = 3
LINE = 8
CHUNK = 4
MESH = pl.DeviceIdType.MESH
NT_DIMS = (((1,), (1,)), ((), ()))
F32 = jnp.float32
BF16 = jnp.bfloat16
NEG = -1e30


def fused(
    cfg,
    x_hbm,
    ids_hbm,
    gates_hbm,
    grad_hbm,
    k_hbm,
    v_hbm,
    q_hbm,
    wg_hbm,
    wu_hbm,
    wd_hbm,
    attn_hbm,
    mo_ref,
    mg_ref,
    wg,
    wu,
    wd,
    qbuf,
    kbuf,
    vbuf,
    obuf,
    m_s,
    l_s,
    acc_s,
    idsg,
    gatesg,
    xg,
    gg,
    sel_s,
    selg_s,
    sx,
    sg,
    rx,
    rg,
    so,
    si,
    bo,
    bi,
    po_s,
    pi_s,
    po_r,
    pi,
    line_send,
    line_recv,
    kv_send,
    kv_recv,
    pair_send,
    pair_recv,
    local_sem,
):
    n_group, line, tok, topk, chunk = cfg
    chips = n_group // 2
    rows = line * CAP * line
    part = CAP * line
    width = x_hbm.shape[1]
    g = lax.axis_index("group")
    seq = lax.axis_index("seq")
    tp = lax.axis_index("tp")
    core = lax.rem(g, 2)
    chip = g // 2
    y = lax.rem(seq, line)
    z = (seq // line) * 2 + tp
    a = z + core * (y - z)
    b = y + core * (z - y)

    def peer(aa, bb):
        yy = bb + core * (aa - bb)
        zz = aa + core * (bb - aa)
        return (g, (zz // 2) * line + yy, lax.rem(zz, 2))

    def in_group(j):
        return (j, seq, tp)

    other = 1 - core
    sibling = in_group(2 * chip + other)

    barrier = pltpu.get_barrier_semaphore()

    def greet_line(i, carry):
        pl.semaphore_signal(barrier, 1, device_id=peer(lax.rem(a + i, line), b), device_id_type=MESH)
        pl.semaphore_signal(barrier, 1, device_id=peer(a, lax.rem(b + i, line)), device_id_type=MESH)
        return carry

    lax.fori_loop(1, line, greet_line, 0)

    def greet_group(i, carry):
        pl.semaphore_signal(
            barrier, 1, device_id=in_group(lax.rem(g + i, n_group)), device_id_type=MESH
        )
        return carry

    lax.fori_loop(1, n_group, greet_group, 0)

    half = qbuf.shape[2]
    mine = pl.ds(pl.multiple_of(core * half, half), half)
    theirs = pl.ds(pl.multiple_of(other * half, half), half)
    head = pl.ds(pl.multiple_of(core * HD, HD), HD)
    early = [
        pltpu.make_async_copy(ids_hbm, idsg.at[a], local_sem.at[0]),
        pltpu.make_async_copy(gates_hbm, gatesg.at[a], local_sem.at[1]),
        pltpu.make_async_copy(x_hbm, xg.at[a], local_sem.at[2]),
        pltpu.make_async_copy(grad_hbm, gg.at[a], local_sem.at[3]),
    ]
    own_heads = [
        pltpu.make_async_copy(q_hbm.at[:, mine], qbuf.at[core], local_sem.at[4]),
        pltpu.make_async_copy(k_hbm.at[:, head], kbuf.at[g], local_sem.at[5]),
        pltpu.make_async_copy(v_hbm.at[:, head], vbuf.at[g], local_sem.at[6]),
    ]
    loads = [
        pltpu.make_async_copy(wg_hbm, wg, local_sem.at[7]),
        pltpu.make_async_copy(wu_hbm, wu, local_sem.at[8]),
        pltpu.make_async_copy(wd_hbm, wd, local_sem.at[9]),
    ]
    for load in early + own_heads + loads:
        load.start()

    @pl.when((lax.rem(chip, 2) == 0) & (chunk > 2))
    def _():
        for extra in range(2, chunk):
            kbuf[2 * chip + extra] = jnp.zeros(kbuf.shape[1:], BF16)
            vbuf[2 * chip + extra] = jnp.zeros(vbuf.shape[1:], BF16)

    pl.semaphore_wait(barrier, 2 * (line - 1) + n_group - 1)

    def distance(i):
        odd = lax.rem(i, 2)
        return line // 2 + odd * (i // 2) - (1 - odd) * (i // 2)

    def along_a(f, source, dest, i):
        p = lax.rem(a + distance(i), line)
        return pltpu.make_async_remote_copy(
            src_ref=source(p),
            dst_ref=dest.at[a],
            send_sem=line_send.at[f, i],
            recv_sem=line_recv.at[f, a],
            device_id=peer(p, b),
            device_id_type=MESH,
        )

    def along_b(f, source, dest, i):
        p = lax.rem(b + distance(i), line)
        return pltpu.make_async_remote_copy(
            src_ref=source(p),
            dst_ref=dest.at[b],
            send_sem=line_send.at[f, i],
            recv_sem=line_recv.at[f, b],
            device_id=peer(a, p),
            device_id_type=MESH,
        )

    def send_all(copy, f, source, dest):
        def step(i, carry):
            copy(f, source, dest, i).start()
            return carry

        lax.fori_loop(1, line, step, 0)

    def sent_all(copy, f, source, dest):
        def step(i, carry):
            copy(f, source, dest, i).wait_send()
            return carry

        lax.fori_loop(1, line, step, 0)

    def wait_all(f, me, dest):
        def step(i, carry):
            p = lax.rem(me + i, line)
            pltpu.make_async_remote_copy(
                src_ref=dest.at[p],
                dst_ref=dest.at[p],
                send_sem=line_send.at[f, i],
                recv_sem=line_recv.at[f, p],
                device_id=peer(a, b),
                device_id_type=MESH,
            ).wait_recv()
            return carry

        lax.fori_loop(1, line, step, 0)

    send_all(along_a, 0, lambda p: ids_hbm, idsg)
    send_all(along_a, 9, lambda p: gates_hbm, gatesg)
    send_all(along_a, 1, lambda p: x_hbm, xg)

    near = {8: (1, -1, 2, -2), 4: (1, -1, 2), 2: (1,)}[line]
    passed_on = {8: ((-2, 1), (-2, 2), (2, -1))}.get(line, ())

    def at_a(offset):
        return lax.rem(a + offset + line, line)

    def grad_copy(n, source, p, offset):
        return pltpu.make_async_remote_copy(
            src_ref=source,
            dst_ref=gg.at[p],
            send_sem=line_send.at[2, n],
            recv_sem=line_recv.at[2, p],
            device_id=peer(at_a(offset), b),
            device_id_type=MESH,
        )

    def grad_near(n):
        return grad_copy(n, grad_hbm, a, near[n])

    def grad_pass(n):
        p = at_a(passed_on[n][0])
        return grad_copy(len(near) + n, gg.at[p], p, passed_on[n][1])

    def grad_wait(offset):
        p = at_a(offset)
        grad_copy(0, gg.at[p], p, 1).wait_recv()

    for n in range(len(near)):
        grad_near(n).start()

    def kv_copy(j, what, source, dest):
        cols = pl.ds(pl.multiple_of(lax.rem(j, 2) * HD, HD), HD)
        return pltpu.make_async_remote_copy(
            src_ref=source.at[:, cols],
            dst_ref=dest.at[g],
            send_sem=kv_send.at[what, j],
            recv_sem=kv_recv.at[what, g],
            device_id=in_group(j),
            device_id_type=MESH,
        )

    def kv_start(j, carry):
        @pl.when(j != g)
        def _():
            kv_copy(j, 0, k_hbm, kbuf).start()
            kv_copy(j, 1, v_hbm, vbuf).start()

        return carry

    lax.fori_loop(2 * chip, n_group, kv_start, 0)
    q_send = pltpu.make_async_remote_copy(
        src_ref=q_hbm.at[:, theirs],
        dst_ref=qbuf.at[core],
        send_sem=pair_send.at[0],
        recv_sem=pair_recv.at[0],
        device_id=sibling,
        device_id_type=MESH,
    )
    q_send.start()
    for load in early:
        load.wait()

    wait_all(0, a, idsg)
    wait_all(9, a, gatesg)
    n_tok = line * tok
    ids_t = jnp.concatenate([idsg[p] for p in range(line)], axis=1).astype(F32)
    gates_t = jnp.concatenate([gatesg[p] for p in range(line)], axis=1)
    place = lax.broadcasted_iota(jnp.int32, (line, n_tok), 0)
    first = ((a // 2) * line + place) * 2 + lax.rem(a, 2)
    second = ((place // 2) * line + a) * 2 + lax.rem(place, 2)
    expert = (first + core * (second - first)).astype(F32)
    named = jnp.zeros((line, n_tok), F32)
    gate = jnp.zeros((line, n_tok), F32)
    for k in range(topk):
        hit = jnp.where(ids_t[k : k + 1] == expert, 1.0, 0.0)
        named = named + hit
        gate = gate + hit * gates_t[k : k + 1]
    t_row = lax.broadcasted_iota(jnp.int32, (n_tok, n_tok), 0)
    t_col = lax.broadcasted_iota(jnp.int32, (n_tok, n_tok), 1)
    earlier = jnp.where((t_row // tok == t_col // tok) & (t_row < t_col), 1.0, 0.0)
    rank = jnp.dot(named.astype(BF16), earlier.astype(BF16), preferred_element_type=F32)
    own_block = jnp.where(place == lax.broadcasted_iota(jnp.int32, (line, n_tok), 1) // tok, 1.0, 0.0)
    for s in range(CAP):
        slot = jnp.where(rank == s, named, 0.0)
        slot_gate = slot * gate
        for d in range(line):
            at = pl.ds(d * part + s * line, line)
            sel_s[at] = own_block * slot[d : d + 1]
            selg_s[at] = own_block * slot_gate[d : d + 1]
    sel = sel_s[...]
    sel_b = sel.astype(BF16)
    gate_col = jnp.sum(selg_s[...], axis=1, keepdims=True)

    tile = min(width // 2, 512)

    def rows_of(ref, cols):
        return jnp.concatenate(
            [ref[d, s, :, cols].astype(F32) for d in range(line) for s in range(CAP)], axis=0
        ).astype(BF16)

    def put_rows(ref, cols, value):
        for d in range(line):
            for s in range(CAP):
                r = d * part + s * line
                ref[d, s, :, cols] = value[r : r + line].astype(BF16)

    def pick(source, dest, received, scale):
        for c in range(0, width, tile):
            cols = slice(c, c + tile)
            block = source[:, :, cols].reshape(n_tok, tile)
            picked = jnp.dot(sel_b, block, preferred_element_type=F32)
            if scale is not None:
                picked = picked * scale
            put_rows(dest, cols, picked)
        received[b] = dest[b]

    wait_all(1, a, xg)
    pick(xg, sx, rx, None)
    send_all(along_b, 3, lambda p: sx.at[p], rx)
    first_seen = sorted({offset for offset, _ in passed_on})
    for offset in first_seen:
        grad_wait(offset)
    for n in range(len(passed_on)):
        grad_pass(n).start()
    for offset in range(1, line):
        if offset not in [o % line for o in first_seen]:
            grad_wait(offset)
    pick(gg, sg, rg, gate_col)
    send_all(along_b, 4, lambda p: sg.at[p], rg)

    for load in loads:
        load.wait()

    wait_all(3, b, rx)
    ffe = wg.shape[1]
    hgate = jnp.zeros((rows, ffe), F32)
    hup = jnp.zeros((rows, ffe), F32)
    for c in range(0, width, tile):
        cols = slice(c, c + tile)
        token_rows = rows_of(rx, cols)
        hgate = hgate + jnp.dot(token_rows, wg[cols, :], preferred_element_type=F32)
        hup = hup + jnp.dot(token_rows, wu[cols, :], preferred_element_type=F32)
    sig = 1.0 / (1.0 + jnp.exp(-hgate))
    silu = hgate * sig
    act = (silu * hup).astype(BF16)
    for c in range(0, width, tile):
        cols = slice(c, c + tile)
        put_rows(so, cols, jnp.dot(act, wd[:, cols], preferred_element_type=F32))
    bo[b] = so[b]
    send_all(along_b, 5, lambda p: so.at[p], bo)

    n_heads = half // HD
    pos = k_hbm.shape[0]
    q_rows = 2 * pos
    keys = chunk * pos
    exp_scale = 1.4426950408889634 / HD**0.5
    n_chunks = (2 * chip + 1 + chunk) // chunk

    def kv_wait(j):
        @pl.when((j != g) & (j < 2 * chip + 2))
        def _():
            for what, dest in ((0, kbuf), (1, vbuf)):
                pltpu.make_async_remote_copy(
                    src_ref=dest.at[j],
                    dst_ref=dest.at[j],
                    send_sem=kv_send.at[what, j],
                    recv_sem=kv_recv.at[what, j],
                    device_id=sibling,
                    device_id_type=MESH,
                ).wait_recv()

    def attend(j, diagonal):
        def arrived(t, carry):
            kv_wait(j * chunk + t)
            return carry

        lax.fori_loop(0, chunk, arrived, 0)
        key_rows = kbuf[pl.ds(j * chunk, chunk)].reshape(keys, HD)
        value_rows = vbuf[pl.ds(j * chunk, chunk)].reshape(keys, HD)
        if diagonal:
            ahead = lax.broadcasted_iota(jnp.int32, (q_rows, keys), 1) - lax.broadcasted_iota(
                jnp.int32, (q_rows, keys), 0
            )
            seen = ahead <= q_rows * chip - keys * j
        for h in range(n_heads):
            cols = slice(h * HD, (h + 1) * HD)
            query_rows = qbuf[:, :, cols].reshape(q_rows, HD)
            scores = lax.dot_general(query_rows, key_rows, NT_DIMS, preferred_element_type=F32)
            if diagonal:
                scores = jnp.where(seen, scores, NEG)
            top = jnp.max(scores, axis=1, keepdims=True)
            m_new = jnp.broadcast_to(top, (q_rows, HD)) if diagonal else jnp.maximum(m_s[h], top)
            total = None
            weights = []
            for c in range(0, keys, HD):
                e = jnp.exp2((scores[:, c : c + HD] - m_new) * exp_scale)
                total = e if total is None else total + e
                weights.append(e.astype(BF16))
            mixed = jnp.dot(jnp.concatenate(weights, axis=1), value_rows, preferred_element_type=F32)
            if not diagonal:
                alpha = jnp.exp2((m_s[h] - m_new) * exp_scale)
                total = total + alpha * l_s[h]
                mixed = mixed + alpha * acc_s[h]
            m_s[h] = m_new
            l_s[h] = total
            acc_s[h] = mixed

    def attend_down(first, last):
        def step(i, carry):
            attend(n_chunks - 1 - i, False)
            return carry

        lax.fori_loop(first, last, step, 0)

    for load in own_heads:
        load.wait()
    q_send.wait_recv()
    attend(n_chunks - 1, True)
    attend_down(1, jnp.minimum(n_chunks, 2))

    wait_all(4, b, rg)
    grad_act = jnp.zeros((rows, ffe), F32)
    for c in range(0, width, tile):
        cols = slice(c, c + tile)
        grad_act = grad_act + lax.dot_general(
            rows_of(rg, cols), wd[:, cols], NT_DIMS, preferred_element_type=F32
        )
    grad_gate = (grad_act * hup * sig * (1.0 + hgate * (1.0 - sig))).astype(BF16)
    grad_up = (grad_act * silu).astype(BF16)
    wide = width // 2
    for h in range(2):
        for c in range(0, wide, tile):
            cols = slice(h * wide + c, h * wide + c + tile)
            put_rows(
                si.at[h],
                slice(c, c + tile),
                lax.dot_general(grad_gate, wg[cols, :], NT_DIMS, preferred_element_type=F32)
                + lax.dot_general(grad_up, wu[cols, :], NT_DIMS, preferred_element_type=F32),
            )
        bi[h, b] = si[h, b]
        send_all(along_b, (6, 10)[h], lambda p, h=h: si.at[h, p], bi.at[h])

    attend_down(2, n_chunks)
    for h in range(n_heads):
        cols = slice(h * HD, (h + 1) * HD)
        done = acc_s[h] / jnp.sum(l_s[h], axis=1, keepdims=True)
        obuf[:, :, cols] = done.astype(BF16).reshape(2, pos, HD)
    o_send = pltpu.make_async_remote_copy(
        src_ref=obuf.at[other],
        dst_ref=attn_hbm.at[:, mine],
        send_sem=pair_send.at[1],
        recv_sem=pair_recv.at[1],
        device_id=sibling,
        device_id_type=MESH,
    )
    o_send.start()
    o_store = pltpu.make_async_copy(obuf.at[core], attn_hbm.at[:, mine], local_sem.at[4])
    o_store.start()

    gated_hi = selg_s[...].astype(BF16)
    gated_lo = (selg_s[...] - gated_hi.astype(F32)).astype(BF16)
    hi_t = gated_hi.astype(F32).T.astype(BF16)
    lo_t = gated_lo.astype(F32).T.astype(BF16)
    sel_t = sel.T.astype(BF16)

    def mix(returned, dest, lefts):
        for c in range(0, returned.shape[-1], tile):
            cols = slice(c, c + tile)
            block = rows_of(returned, cols)
            mixed = jnp.dot(lefts[0], block, preferred_element_type=F32)
            for left in lefts[1:]:
                mixed = mixed + jnp.dot(left, block, preferred_element_type=F32)
            dest[:, :, cols] = mixed.astype(BF16).reshape(line, tok, tile)

    sums = {
        8: ((0, 1, 1), (1, -1, -1), (2, -3, -1), (3, 4, -2), (4, 3, 1)),
        4: ((0, 1, 1), (1, -1, -1), (2, 2, 2)),
        2: ((0, 1, 1),),
    }[line]
    added = {8: ((5, -2, (2, 3)), (6, 2, (4,)))}.get(line, ())
    half_way = [t for _, _, slots in added for t in slots]

    def sum_copy(slot, home, offset):
        return pltpu.make_async_remote_copy(
            src_ref=po_s.at[at_a(home)],
            dst_ref=po_r.at[slot],
            send_sem=line_send.at[7, slot],
            recv_sem=line_recv.at[7, slot],
            device_id=peer(at_a(offset), b),
            device_id_type=MESH,
        )

    wait_all(5, b, bo)
    mix(bo, po_s, (hi_t, lo_t))
    for slot, home, offset in sums:
        sum_copy(slot, home, offset).start()

    for h in range(2):
        wait_all((6, 10)[h], b, bi.at[h])
        mix(bi.at[h], pi_s.at[h], (sel_t,))
        pi[h, a] = pi_s[h, a]
        send_all(along_a, (8, 11)[h], lambda p, h=h: pi_s.at[h, p], pi.at[h])

    for slot, home, slots in added:
        total = po_s[at_a(home)].astype(F32)
        for t in slots:
            sum_copy(t, 0, 1).wait_recv()
            total = total + po_r[t].astype(F32)
        po_s[at_a(home)] = total.astype(BF16)
        sum_copy(slot, home, home).start()
    total = po_s[a].astype(F32)
    for slot in [m[0] for m in sums] + [m[0] for m in added]:
        if slot not in half_way:
            sum_copy(slot, 0, 1).wait_recv()
            total = total + po_r[slot].astype(F32)
    mo_ref[...] = total.astype(BF16)

    for h in range(2):
        wait_all((8, 11)[h], a, pi.at[h])
        total = pi[h, 0].astype(F32)
        for p in range(1, line):
            total = total + pi[h, p].astype(F32)
        mg_ref[:, h * wide : (h + 1) * wide] = total.astype(BF16)

    o_store.wait()
    o_send.wait()
    q_send.wait_send()
    sent_all(along_a, 0, lambda p: ids_hbm, idsg)
    sent_all(along_a, 9, lambda p: gates_hbm, gatesg)
    sent_all(along_a, 1, lambda p: x_hbm, xg)
    sent_all(along_b, 3, lambda p: sx.at[p], rx)
    sent_all(along_b, 4, lambda p: sg.at[p], rg)
    sent_all(along_b, 5, lambda p: so.at[p], bo)
    for h in range(2):
        sent_all(along_b, (6, 10)[h], lambda p, h=h: si.at[h, p], bi.at[h])
        sent_all(along_a, (8, 11)[h], lambda p, h=h: pi_s.at[h, p], pi.at[h])
    for n in range(len(near)):
        grad_near(n).wait_send()
    for n in range(len(passed_on)):
        grad_pass(n).wait_send()
    for slot, home, offset in sums:
        sum_copy(slot, home, offset).wait_send()
    for slot, home, _ in added:
        sum_copy(slot, home, home).wait_send()

    def kv_sent(j, carry):
        @pl.when(j != g)
        def _():
            kv_copy(j, 0, k_hbm, kbuf).wait_send()
            kv_copy(j, 1, v_hbm, vbuf).wait_send()

        return carry

    lax.fori_loop(2 * chip, n_group, kv_sent, 0)


def hand_over(pieces, attn, out, grad_in, attn_o, out_o, grad_o, attn_v, out_v, grad_v, came, went):
    n = attn.shape[0] // pieces
    parts = [
        (attn.at[i * n : i * n + n], attn_v.at[i * n : i * n + n], attn_o.at[i * n : i * n + n])
        for i in range(pieces)
    ] + [(out, out_v, out_o), (grad_in, grad_v, grad_o)]
    reads = [pltpu.make_async_copy(r, v, came.at[i]) for i, (r, v, _) in enumerate(parts)]
    writes = [pltpu.make_async_copy(v, w, went.at[i]) for i, (_, v, w) in enumerate(parts)]
    for read in reads:
        read.start()
    for read, write in zip(reads, writes):
        read.wait()
        write.start()
    for write in writes:
        write.wait()


def shards(queries, keys, values, moe_x, expert_ids, gates, grad_out, w_gate, w_up, w_down):
    n_group = lax.axis_size("group")
    line = LINE
    pos, q_width = queries.shape[1:]
    tok, width = moe_x.shape[1:]
    topk = expert_ids.shape[2]
    ffe = w_gate.shape[2]
    half = q_width // 2
    n_heads = half // HD
    rows = line * CAP * line
    n_tok = line * tok
    chunk = min(CHUNK, n_group)
    vmem = pl.BlockSpec(memory_space=pltpu.VMEM)
    hbm = pl.BlockSpec(memory_space=pl.ANY)
    slots = pltpu.VMEM((line, CAP, line, width), BF16)
    slot_halves = pltpu.VMEM((2, line, CAP, line, width // 2), BF16)
    block = pltpu.VMEM((line, tok, width), BF16)
    halves = pltpu.VMEM((2, line, tok, width // 2), BF16)
    state = pltpu.VMEM((n_heads, 2 * pos, HD), F32)
    attn, out, grad_in = pl.pallas_call(
        functools.partial(fused, (n_group, line, tok, topk, chunk)),
        out_shape=(
            jax.ShapeDtypeStruct((pos, q_width), BF16),
            jax.ShapeDtypeStruct((tok, width), BF16),
            jax.ShapeDtypeStruct((tok, width), BF16),
        ),
        in_specs=[hbm] * 10,
        out_specs=(hbm, vmem, vmem),
        scratch_shapes=[
            pltpu.VMEM((width, ffe), BF16),
            pltpu.VMEM((width, ffe), BF16),
            pltpu.VMEM((ffe, width), BF16),
            pltpu.VMEM((2, pos, half), BF16),
            pltpu.VMEM((n_group, pos, HD), BF16),
            pltpu.VMEM((n_group, pos, HD), BF16),
            pltpu.VMEM((2, pos, half), BF16),
            state,
            state,
            state,
            pltpu.VMEM((line, topk, tok), jnp.int32),
            pltpu.VMEM((line, topk, tok), F32),
            block,
            block,
            pltpu.VMEM((rows, n_tok), F32),
            pltpu.VMEM((rows, n_tok), F32),
        ]
        + [slots] * 5
        + [slot_halves, slots, slot_halves]
        + [block, halves, block, halves]
        + [
            pltpu.SemaphoreType.DMA((12, line)),
            pltpu.SemaphoreType.DMA((12, line)),
            pltpu.SemaphoreType.DMA((2, n_group)),
            pltpu.SemaphoreType.DMA((2, n_group)),
            pltpu.SemaphoreType.DMA((2,)),
            pltpu.SemaphoreType.DMA((2,)),
            pltpu.SemaphoreType.DMA((10,)),
        ],
        compiler_params=pltpu.CompilerParams(
            collective_id=0, has_side_effects=True, vmem_limit_bytes=60 * 1024 * 1024
        ),
    )(
        moe_x[0],
        expert_ids[0].T,
        gates[0].T,
        grad_out[0],
        keys[0],
        values[0],
        queries[0],
        w_gate[0],
        w_up[0],
        w_down[0],
    )
    pieces = 4
    attn, out, grad_in = pl.pallas_call(
        functools.partial(hand_over, pieces),
        out_shape=tuple(jax.ShapeDtypeStruct(t.shape, BF16) for t in (attn, out, grad_in)),
        in_specs=[hbm] * 3,
        out_specs=(hbm,) * 3,
        scratch_shapes=[
            pltpu.VMEM(attn.shape, BF16),
            pltpu.VMEM(out.shape, BF16),
            pltpu.VMEM(out.shape, BF16),
            pltpu.SemaphoreType.DMA((pieces + 2,)),
            pltpu.SemaphoreType.DMA((pieces + 2,)),
        ],
    )(attn, out, grad_in)
    return attn[None], out[None], grad_in[None]


def solution(mesh):
    tokens = P("group", ("seq", "tp"), None)
    heads = P("seq", "group", "tp")
    weights = P(("seq", "tp"), None, None)
    return jax.shard_map(
        shards,
        mesh=mesh,
        in_specs=(heads,) * 3 + (tokens,) * 4 + (weights,) * 3,
        out_specs=(heads, tokens, tokens),
        check_vma=False,
    )
```

```python
import functools

import jax
import jax.numpy as jnp
from jax import lax
from jax.experimental import pallas as pl
from jax.experimental.pallas import tpu as pltpu
from jax.sharding import PartitionSpec as P

H = 32
KVH = 4
HD = 128
CAP = 3
LINE = 8
CHUNK = 4
MESH = pl.DeviceIdType.MESH
NT_DIMS = (((1,), (1,)), ((), ()))
F32 = jnp.float32
BF16 = jnp.bfloat16
NEG = -1e30
FAMILIES = 10


def fused(
    cfg,
    x_hbm,
    ids_hbm,
    gates_hbm,
    grad_hbm,
    k_hbm,
    v_hbm,
    q_hbm,
    wg_hbm,
    wu_hbm,
    wd_hbm,
    attn_hbm,
    mo_ref,
    mg_ref,
    wg,
    wu,
    wd,
    qbuf,
    kbuf,
    vbuf,
    obuf,
    m_s,
    l_s,
    acc_s,
    idsg,
    gatesg,
    xg,
    gg,
    sel_s,
    selg_s,
    sx,
    sg,
    rx,
    rg,
    so,
    si,
    bo,
    bi,
    po_s,
    pi_s,
    po_r,
    pi,
    line_send,
    line_recv,
    kv_send,
    kv_recv,
    pair_send,
    pair_recv,
    local_sem,
):
    n_group, line, tok, topk, chunk = cfg
    chips = n_group // 2
    rows = line * CAP * line
    part = CAP * line
    width = x_hbm.shape[1]
    wide = width // 2
    halves = (0, 1)
    cols_of = [slice(h * wide, (h + 1) * wide) for h in halves]
    g = lax.axis_index("group")
    seq = lax.axis_index("seq")
    tp = lax.axis_index("tp")
    core = lax.rem(g, 2)
    chip = g // 2
    y = lax.rem(seq, line)
    z = (seq // line) * 2 + tp
    me_a = (z, y)
    me_b = (y, z)

    def at(yy, zz):
        return (g, (zz // 2) * line + yy, lax.rem(zz, 2))

    def a_peer(h, p):
        return at(p, z) if h else at(y, p)

    def b_peer(h, p):
        return at(y, p) if h else at(p, z)

    def in_group(j):
        return (j, seq, tp)

    other = 1 - core
    sibling = in_group(2 * chip + other)

    barrier = pltpu.get_barrier_semaphore()

    def greet_line(i, carry):
        for h in halves:
            p = lax.rem(me_a[h] + i, line)
            pl.semaphore_signal(barrier, 1, device_id=a_peer(h, p), device_id_type=MESH)
        return carry

    lax.fori_loop(1, line, greet_line, 0)

    def greet_group(i, carry):
        pl.semaphore_signal(
            barrier, 1, device_id=in_group(lax.rem(g + i, n_group)), device_id_type=MESH
        )
        return carry

    lax.fori_loop(1, n_group, greet_group, 0)

    half = qbuf.shape[2]
    mine = pl.ds(pl.multiple_of(core * half, half), half)
    theirs = pl.ds(pl.multiple_of(other * half, half), half)
    head = pl.ds(pl.multiple_of(core * HD, HD), HD)
    early = []
    for h in halves:
        early += [
            pltpu.make_async_copy(ids_hbm, idsg.at[h, me_a[h]], local_sem.at[6 + 4 * h]),
            pltpu.make_async_copy(gates_hbm, gatesg.at[h, me_a[h]], local_sem.at[7 + 4 * h]),
            pltpu.make_async_copy(x_hbm.at[:, cols_of[h]], xg.at[h, me_a[h]], local_sem.at[8 + 4 * h]),
            pltpu.make_async_copy(grad_hbm.at[:, cols_of[h]], gg.at[h, me_a[h]], local_sem.at[9 + 4 * h]),
        ]
    own_heads = [
        pltpu.make_async_copy(q_hbm.at[:, mine], qbuf.at[core], local_sem.at[0]),
        pltpu.make_async_copy(k_hbm.at[:, head], kbuf.at[g], local_sem.at[1]),
        pltpu.make_async_copy(v_hbm.at[:, head], vbuf.at[g], local_sem.at[2]),
    ]
    loads = [
        pltpu.make_async_copy(wg_hbm, wg, local_sem.at[3]),
        pltpu.make_async_copy(wu_hbm, wu, local_sem.at[4]),
        pltpu.make_async_copy(wd_hbm, wd, local_sem.at[5]),
    ]
    for load in early + own_heads + loads:
        load.start()

    @pl.when((lax.rem(chip, 2) == 0) & (chunk > 2))
    def _():
        for extra in range(2, chunk):
            kbuf[2 * chip + extra] = jnp.zeros(kbuf.shape[1:], BF16)
            vbuf[2 * chip + extra] = jnp.zeros(vbuf.shape[1:], BF16)

    pl.semaphore_wait(barrier, 2 * (line - 1) + n_group - 1)

    def distance(i):
        odd = lax.rem(i, 2)
        return line // 2 + odd * (i // 2) - (1 - odd) * (i // 2)

    def line_copy(on_a, f, source, dest, h, i):
        me = me_a[h] if on_a else me_b[h]
        p = lax.rem(me + distance(i), line)
        return pltpu.make_async_remote_copy(
            src_ref=source(h, p),
            dst_ref=dest.at[h, me],
            send_sem=line_send.at[FAMILIES * h + f, i],
            recv_sem=line_recv.at[FAMILIES * h + f, me],
            device_id=(a_peer if on_a else b_peer)(h, p),
            device_id_type=MESH,
        )

    def send_all(on_a, f, source, dest, which=halves):
        def step(i, carry):
            for h in which:
                line_copy(on_a, f, source, dest, h, i).start()
            return carry

        lax.fori_loop(1, line, step, 0)

    def sent_all(on_a, f, source, dest):
        def step(i, carry):
            for h in halves:
                line_copy(on_a, f, source, dest, h, i).wait_send()
            return carry

        lax.fori_loop(1, line, step, 0)

    def wait_all(on_a, f, dest, h):
        me = me_a[h] if on_a else me_b[h]

        def step(i, carry):
            p = lax.rem(me + i, line)
            pltpu.make_async_remote_copy(
                src_ref=dest.at[h, p],
                dst_ref=dest.at[h, p],
                send_sem=line_send.at[FAMILIES * h + f, i],
                recv_sem=line_recv.at[FAMILIES * h + f, p],
                device_id=sibling,
                device_id_type=MESH,
            ).wait_recv()
            return carry

        lax.fori_loop(1, line, step, 0)

    def ids_from(h, p):
        return ids_hbm

    def gates_from(h, p):
        return gates_hbm

    def x_from(h, p):
        return x_hbm.at[:, cols_of[h]]

    def block_of(ref):
        return lambda h, p: ref.at[h, p]

    send_all(True, 0, ids_from, idsg)
    send_all(True, 9, gates_from, gatesg)
    send_all(True, 1, x_from, xg)

    near = {8: (4, 3, -3, 2, -2, 1, -1), 4: (1, -1, 2), 2: (1,)}[line]
    passed_on = ()

    def at_a(h, offset):
        return lax.rem(me_a[h] + offset + line, line)

    def grad_copy(h, n, source, p, offset):
        return pltpu.make_async_remote_copy(
            src_ref=source,
            dst_ref=gg.at[h, p],
            send_sem=line_send.at[FAMILIES * h + 2, n],
            recv_sem=line_recv.at[FAMILIES * h + 2, p],
            device_id=a_peer(h, at_a(h, offset)),
            device_id_type=MESH,
        )

    def grad_near(h, n):
        return grad_copy(h, n, grad_hbm.at[:, cols_of[h]], me_a[h], near[n])

    def grad_pass(h, n):
        p = at_a(h, passed_on[n][0])
        return grad_copy(h, len(near) + n, gg.at[h, p], p, passed_on[n][1])

    def grad_wait(h, offset):
        p = at_a(h, offset)
        grad_copy(h, 0, gg.at[h, p], p, 1).wait_recv()

    for n in range(len(near)):
        for h in halves:
            grad_near(h, n).start()

    def kv_copy(j, what, source, dest):
        cols = pl.ds(pl.multiple_of(lax.rem(j, 2) * HD, HD), HD)
        return pltpu.make_async_remote_copy(
            src_ref=source.at[:, cols],
            dst_ref=dest.at[g],
            send_sem=kv_send.at[what, j],
            recv_sem=kv_recv.at[what, g],
            device_id=in_group(j),
            device_id_type=MESH,
        )

    def kv_start(j, carry):
        @pl.when(j != g)
        def _():
            kv_copy(j, 0, k_hbm, kbuf).start()
            kv_copy(j, 1, v_hbm, vbuf).start()

        return carry

    lax.fori_loop(2 * chip, n_group, kv_start, 0)
    q_send = pltpu.make_async_remote_copy(
        src_ref=q_hbm.at[:, theirs],
        dst_ref=qbuf.at[core],
        send_sem=pair_send.at[0],
        recv_sem=pair_recv.at[0],
        device_id=sibling,
        device_id_type=MESH,
    )
    q_send.start()
    for load in early:
        load.wait()

    n_tok = line * tok
    place = lax.broadcasted_iota(jnp.int32, (line, n_tok), 0)
    t_row = lax.broadcasted_iota(jnp.int32, (n_tok, n_tok), 0)
    t_col = lax.broadcasted_iota(jnp.int32, (n_tok, n_tok), 1)
    earlier = jnp.where((t_row // tok == t_col // tok) & (t_row < t_col), 1.0, 0.0).astype(BF16)
    own_block = jnp.where(place == lax.broadcasted_iota(jnp.int32, (line, n_tok), 1) // tok, 1.0, 0.0)
    experts = (
        ((z // 2) * line + place) * 2 + lax.rem(z, 2),
        ((place // 2) * line + y) * 2 + lax.rem(place, 2),
    )
    for h in halves:
        wait_all(True, 0, idsg, h)
        wait_all(True, 9, gatesg, h)
        ids_t = jnp.concatenate([idsg[h, p] for p in range(line)], axis=1)
        gates_t = jnp.concatenate([gatesg[h, p] for p in range(line)], axis=1)
        named = jnp.zeros((line, n_tok), F32)
        gate = jnp.zeros((line, n_tok), F32)
        for k in range(topk):
            hit = jnp.where(ids_t[k : k + 1] == experts[h], 1.0, 0.0)
            named = named + hit
            gate = gate + hit * gates_t[k : k + 1]
        rank = jnp.dot(named.astype(BF16), earlier, preferred_element_type=F32)
        for s in range(CAP):
            slot = jnp.where(rank == s, named, 0.0)
            slot_gate = slot * gate
            for d in range(line):
                r = pl.ds(d * part + s * line, line)
                sel_s[h, r] = own_block * slot[d : d + 1]
                selg_s[h, r] = own_block * slot_gate[d : d + 1]

    shift = lax.broadcasted_iota(jnp.int32, (line, rows), 1) - part * lax.broadcasted_iota(
        jnp.int32, (line, rows), 0
    )
    swap = jnp.concatenate(
        [jnp.where(shift == s * line + d, 1.0, 0.0) for d in range(line) for s in range(CAP)], axis=0
    ).astype(BF16)

    def swapped(value):
        return jnp.dot(swap, value, preferred_element_type=F32).astype(BF16)

    tile = min(wide, 512)

    def rows_of(ref, h, cols):
        return jnp.concatenate(
            [ref[h, d, s, :, cols].astype(F32) for d in range(line) for s in range(CAP)], axis=0
        ).astype(BF16)

    def put_rows(ref, h, cols, value):
        for d in range(line):
            for s in range(CAP):
                r = d * part + s * line
                ref[h, d, s, :, cols] = value[r : r + line].astype(BF16)

    def pick(h, source, dest, received, scaled):
        left = sel_s[h].astype(BF16)
        if scaled:
            scale = jnp.sum(selg_s[h], axis=1, keepdims=True)
        for c in range(0, wide, tile):
            cols = slice(c, c + tile)
            block = source[h, :, :, cols].reshape(n_tok, tile)
            picked = jnp.dot(left, block, preferred_element_type=F32)
            if scaled:
                picked = picked * scale
            put_rows(dest, h, cols, picked)
        received[h, me_b[h]] = dest[h, me_b[h]]

    wait_all(True, 1, xg, 0)
    first_seen = sorted({offset for offset, _ in passed_on})
    for h in halves:
        for offset in first_seen:
            grad_wait(h, offset)
        for n in range(len(passed_on)):
            grad_pass(h, n).start()

    for h in halves:
        if h:
            wait_all(True, 1, xg, h)
        pick(h, xg, sx, rx, False)
        send_all(False, 3, block_of(sx), rx, (h,))

    for h in halves:
        for offset in range(1, line):
            if offset not in [o % line for o in first_seen]:
                grad_wait(h, offset)
        pick(h, gg, sg, rg, True)
        send_all(False, 4, block_of(sg), rg, (h,))

    for load in loads:
        load.wait()

    ffe = wg.shape[1]
    hgate = jnp.zeros((rows, ffe), F32)
    hup = jnp.zeros((rows, ffe), F32)
    for h in halves:
        wait_all(False, 3, rx, h)
        for c in range(0, wide, tile):
            token_rows = rows_of(rx, h, slice(c, c + tile))
            if h:
                token_rows = swapped(token_rows)
            depth = slice(h * wide + c, h * wide + c + tile)
            hgate = hgate + jnp.dot(token_rows, wg[depth, :], preferred_element_type=F32)
            hup = hup + jnp.dot(token_rows, wu[depth, :], preferred_element_type=F32)
    sig = 1.0 / (1.0 + jnp.exp(-hgate))
    silu = hgate * sig
    act = (silu * hup).astype(BF16)
    for h in halves:
        left = swapped(act) if h else act
        for c in range(0, wide, tile):
            depth = slice(h * wide + c, h * wide + c + tile)
            put_rows(
                so, h, slice(c, c + tile), jnp.dot(left, wd[:, depth], preferred_element_type=F32)
            )
        bo[h, me_b[h]] = so[h, me_b[h]]
        send_all(False, 5, block_of(so), bo, (h,))

    n_heads = half // HD
    pos = k_hbm.shape[0]
    q_rows = 2 * pos
    keys = chunk * pos
    exp_scale = 1.4426950408889634 / HD**0.5
    n_chunks = (2 * chip + 1 + chunk) // chunk

    def kv_wait(j):
        @pl.when((j != g) & (j < 2 * chip + 2))
        def _():
            for what, dest in ((0, kbuf), (1, vbuf)):
                pltpu.make_async_remote_copy(
                    src_ref=dest.at[j],
                    dst_ref=dest.at[j],
                    send_sem=kv_send.at[what, j],
                    recv_sem=kv_recv.at[what, j],
                    device_id=sibling,
                    device_id_type=MESH,
                ).wait_recv()

    def attend(j, diagonal):
        def arrived(t, carry):
            kv_wait(j * chunk + t)
            return carry

        lax.fori_loop(0, chunk, arrived, 0)
        key_rows = kbuf[pl.ds(j * chunk, chunk)].reshape(keys, HD)
        value_rows = vbuf[pl.ds(j * chunk, chunk)].reshape(keys, HD)
        if diagonal:
            ahead = lax.broadcasted_iota(jnp.int32, (q_rows, keys), 1) - lax.broadcasted_iota(
                jnp.int32, (q_rows, keys), 0
            )
            seen = ahead <= q_rows * chip - keys * j
        for h in range(n_heads):
            cols = slice(h * HD, (h + 1) * HD)
            query_rows = qbuf[:, :, cols].reshape(q_rows, HD)
            scores = lax.dot_general(query_rows, key_rows, NT_DIMS, preferred_element_type=F32)
            if diagonal:
                scores = jnp.where(seen, scores, NEG)
            top = jnp.max(scores, axis=1, keepdims=True)
            m_new = jnp.broadcast_to(top, (q_rows, HD)) if diagonal else jnp.maximum(m_s[h], top)
            total = None
            weights = []
            for c in range(0, keys, HD):
                e = jnp.exp2((scores[:, c : c + HD] - m_new) * exp_scale)
                total = e if total is None else total + e
                weights.append(e.astype(BF16))
            mixed = jnp.dot(jnp.concatenate(weights, axis=1), value_rows, preferred_element_type=F32)
            if not diagonal:
                alpha = jnp.exp2((m_s[h] - m_new) * exp_scale)
                total = total + alpha * l_s[h]
                mixed = mixed + alpha * acc_s[h]
            m_s[h] = m_new
            l_s[h] = total
            acc_s[h] = mixed

    def attend_down(first, last):
        def step(i, carry):
            attend(n_chunks - 1 - i, False)
            return carry

        lax.fori_loop(first, last, step, 0)

    for load in own_heads:
        load.wait()
    q_send.wait_recv()
    attend(n_chunks - 1, True)
    attend_down(1, jnp.minimum(n_chunks, 2))

    grad_act = jnp.zeros((rows, ffe), F32)
    for h in halves:
        wait_all(False, 4, rg, h)
        for c in range(0, wide, tile):
            grad_rows = rows_of(rg, h, slice(c, c + tile))
            if h:
                grad_rows = swapped(grad_rows)
            depth = slice(h * wide + c, h * wide + c + tile)
            grad_act = grad_act + lax.dot_general(
                grad_rows, wd[:, depth], NT_DIMS, preferred_element_type=F32
            )
    grad_gate = (grad_act * hup * sig * (1.0 + hgate * (1.0 - sig))).astype(BF16)
    grad_up = (grad_act * silu).astype(BF16)
    for h in halves:
        if h:
            grad_gate, grad_up = swapped(grad_gate), swapped(grad_up)
        for c in range(0, wide, tile):
            depth = slice(h * wide + c, h * wide + c + tile)
            put_rows(
                si,
                h,
                slice(c, c + tile),
                lax.dot_general(grad_gate, wg[depth, :], NT_DIMS, preferred_element_type=F32)
                + lax.dot_general(grad_up, wu[depth, :], NT_DIMS, preferred_element_type=F32),
            )
        bi[h, me_b[h]] = si[h, me_b[h]]
        send_all(False, 6, block_of(si), bi, (h,))

    attend_down(2, n_chunks)
    for h in range(n_heads):
        cols = slice(h * HD, (h + 1) * HD)
        done = acc_s[h] / jnp.sum(l_s[h], axis=1, keepdims=True)
        obuf[:, :, cols] = done.astype(BF16).reshape(2, pos, HD)
    o_send = pltpu.make_async_remote_copy(
        src_ref=obuf.at[other],
        dst_ref=attn_hbm.at[:, mine],
        send_sem=pair_send.at[1],
        recv_sem=pair_recv.at[1],
        device_id=sibling,
        device_id_type=MESH,
    )
    o_send.start()
    o_store = pltpu.make_async_copy(obuf.at[core], attn_hbm.at[:, mine], local_sem.at[0])
    o_store.start()

    def mix(h, returned, dest, lefts):
        for c in range(0, wide, tile):
            cols = slice(c, c + tile)
            block = rows_of(returned, h, cols)
            mixed = jnp.dot(lefts[0], block, preferred_element_type=F32)
            for left in lefts[1:]:
                mixed = mixed + jnp.dot(left, block, preferred_element_type=F32)
            dest[h, :, :, cols] = mixed.astype(BF16).reshape(line, tok, tile)

    sums = {
        8: ((0, 1, 1), (1, -1, -1), (2, -3, -1), (3, 4, -2), (4, 3, 1)),
        4: ((0, 1, 1), (1, -1, -1), (2, 2, 2)),
        2: ((0, 1, 1),),
    }[line]
    added = {8: ((5, -2, (2, 3)), (6, 2, (4,)))}.get(line, ())
    half_way = [t for _, _, slots in added for t in slots]

    def sum_copy(h, slot, home, offset):
        return pltpu.make_async_remote_copy(
            src_ref=po_s.at[h, at_a(h, home)],
            dst_ref=po_r.at[h, slot],
            send_sem=line_send.at[FAMILIES * h + 7, slot],
            recv_sem=line_recv.at[FAMILIES * h + 7, slot],
            device_id=a_peer(h, at_a(h, offset)),
            device_id_type=MESH,
        )

    for h in halves:
        hi = selg_s[h].astype(BF16).astype(F32)
        lo = selg_s[h] - hi
        wait_all(False, 5, bo, h)
        mix(h, bo, po_s, (hi.T.astype(BF16), lo.T.astype(BF16)))
        for slot, home, offset in sums:
            sum_copy(h, slot, home, offset).start()

    for h in halves:
        wait_all(False, 6, bi, h)
        mix(h, bi, pi_s, (sel_s[h].T.astype(BF16),))
        pi[h, me_a[h]] = pi_s[h, me_a[h]]
        send_all(True, 8, block_of(pi_s), pi, (h,))

    for h in halves:
        for slot, home, slots in added:
            total = po_s[h, at_a(h, home)].astype(F32)
            for t in slots:
                sum_copy(h, t, 0, 1).wait_recv()
                total = total + po_r[h, t].astype(F32)
            po_s[h, at_a(h, home)] = total.astype(BF16)
            sum_copy(h, slot, home, home).start()
    for h in halves:
        total = po_s[h, me_a[h]].astype(F32)
        for slot in [m[0] for m in sums] + [m[0] for m in added]:
            if slot not in half_way:
                sum_copy(h, slot, 0, 1).wait_recv()
                total = total + po_r[h, slot].astype(F32)
        mo_ref[:, cols_of[h]] = total.astype(BF16)

    for h in halves:
        wait_all(True, 8, pi, h)
        total = pi[h, 0].astype(F32)
        for p in range(1, line):
            total = total + pi[h, p].astype(F32)
        mg_ref[:, cols_of[h]] = total.astype(BF16)

    o_store.wait()
    o_send.wait()
    q_send.wait_send()
    sent_all(True, 0, ids_from, idsg)
    sent_all(True, 9, gates_from, gatesg)
    sent_all(True, 1, x_from, xg)
    sent_all(False, 3, block_of(sx), rx)
    sent_all(False, 4, block_of(sg), rg)
    sent_all(False, 5, block_of(so), bo)
    sent_all(False, 6, block_of(si), bi)
    sent_all(True, 8, block_of(pi_s), pi)
    for h in halves:
        for n in range(len(near)):
            grad_near(h, n).wait_send()
        for n in range(len(passed_on)):
            grad_pass(h, n).wait_send()
        for slot, home, offset in sums:
            sum_copy(h, slot, home, offset).wait_send()
        for slot, home, _ in added:
            sum_copy(h, slot, home, home).wait_send()

    def kv_sent(j, carry):
        @pl.when(j != g)
        def _():
            kv_copy(j, 0, k_hbm, kbuf).wait_send()
            kv_copy(j, 1, v_hbm, vbuf).wait_send()

        return carry

    lax.fori_loop(2 * chip, n_group, kv_sent, 0)


def hand_over(pieces, attn, out, grad_in, attn_o, out_o, grad_o, attn_v, out_v, grad_v, came, went):
    n = attn.shape[0] // pieces
    parts = [
        (attn.at[i * n : i * n + n], attn_v.at[i * n : i * n + n], attn_o.at[i * n : i * n + n])
        for i in range(pieces)
    ] + [(out, out_v, out_o), (grad_in, grad_v, grad_o)]
    reads = [pltpu.make_async_copy(r, v, came.at[i]) for i, (r, v, _) in enumerate(parts)]
    writes = [pltpu.make_async_copy(v, w, went.at[i]) for i, (_, v, w) in enumerate(parts)]
    for read in reads:
        read.start()
    for read, write in zip(reads, writes):
        read.wait()
        write.start()
    for write in writes:
        write.wait()


def shards(queries, keys, values, moe_x, expert_ids, gates, grad_out, w_gate, w_up, w_down):
    n_group = lax.axis_size("group")
    line = LINE
    pos, q_width = queries.shape[1:]
    tok, width = moe_x.shape[1:]
    topk = expert_ids.shape[2]
    ffe = w_gate.shape[2]
    half = q_width // 2
    n_heads = half // HD
    rows = line * CAP * line
    n_tok = line * tok
    chunk = min(CHUNK, n_group)
    vmem = pl.BlockSpec(memory_space=pltpu.VMEM)
    hbm = pl.BlockSpec(memory_space=pl.ANY)
    slots = pltpu.VMEM((2, line, CAP, line, width // 2), BF16)
    block = pltpu.VMEM((2, line, tok, width // 2), BF16)
    state = pltpu.VMEM((n_heads, 2 * pos, HD), F32)
    attn, out, grad_in = pl.pallas_call(
        functools.partial(fused, (n_group, line, tok, topk, chunk)),
        out_shape=(
            jax.ShapeDtypeStruct((pos, q_width), BF16),
            jax.ShapeDtypeStruct((tok, width), BF16),
            jax.ShapeDtypeStruct((tok, width), BF16),
        ),
        in_specs=[hbm] * 10,
        out_specs=(hbm, vmem, vmem),
        scratch_shapes=[
            pltpu.VMEM((width, ffe), BF16),
            pltpu.VMEM((width, ffe), BF16),
            pltpu.VMEM((ffe, width), BF16),
            pltpu.VMEM((2, pos, half), BF16),
            pltpu.VMEM((n_group, pos, HD), BF16),
            pltpu.VMEM((n_group, pos, HD), BF16),
            pltpu.VMEM((2, pos, half), BF16),
            state,
            state,
            state,
            pltpu.VMEM((2, line, topk, tok), jnp.int32),
            pltpu.VMEM((2, line, topk, tok), F32),
            block,
            block,
            pltpu.VMEM((2, rows, n_tok), F32),
            pltpu.VMEM((2, rows, n_tok), F32),
        ]
        + [slots] * 8
        + [block] * 4
        + [
            pltpu.SemaphoreType.DMA((2 * FAMILIES, line)),
            pltpu.SemaphoreType.DMA((2 * FAMILIES, line)),
            pltpu.SemaphoreType.DMA((2, n_group)),
            pltpu.SemaphoreType.DMA((2, n_group)),
            pltpu.SemaphoreType.DMA((2,)),
            pltpu.SemaphoreType.DMA((2,)),
            pltpu.SemaphoreType.DMA((14,)),
        ],
        compiler_params=pltpu.CompilerParams(
            collective_id=0, has_side_effects=True, vmem_limit_bytes=60 * 1024 * 1024
        ),
    )(
        moe_x[0],
        expert_ids[0].T,
        gates[0].T,
        grad_out[0],
        keys[0],
        values[0],
        queries[0],
        w_gate[0],
        w_up[0],
        w_down[0],
    )
    pieces = 4
    attn, out, grad_in = pl.pallas_call(
        functools.partial(hand_over, pieces),
        out_shape=tuple(jax.ShapeDtypeStruct(t.shape, BF16) for t in (attn, out, grad_in)),
        in_specs=[hbm] * 3,
        out_specs=(hbm,) * 3,
        scratch_shapes=[
            pltpu.VMEM(attn.shape, BF16),
            pltpu.VMEM(out.shape, BF16),
            pltpu.VMEM(out.shape, BF16),
            pltpu.SemaphoreType.DMA((pieces + 2,)),
            pltpu.SemaphoreType.DMA((pieces + 2,)),
        ],
    )(attn, out, grad_in)
    return attn[None], out[None], grad_in[None]


def solution(mesh):
    tokens = P("group", ("seq", "tp"), None)
    heads = P("seq", "group", "tp")
    weights = P(("seq", "tp"), None, None)
    return jax.shard_map(
        shards,
        mesh=mesh,
        in_specs=(heads,) * 3 + (tokens,) * 4 + (weights,) * 3,
        out_specs=(heads, tokens, tokens),
        check_vma=False,
    )
```
